128 devices in a mesh: curve: 16 (over z, y), sub: 8 (over x, core).
Axes of the slice: x: 4, y: 4, z: 4, core: 2. Of those that a mesh axis runs over, the one named last changes fastest.
Arguments:
- state_old: float32 [32768, 5, 512], P(('curve', 'sub')), as said below
- metric_old: float32 [32768], P(('curve', 'sub')), may hold values from 1 to 4
- new_position: int32 [32768], P(('curve', 'sub')), may hold values from -1 to 16383, as said below
- partner: int32 [6, 16384], P(None, ('curve', 'sub')), may hold values from -1 to 16383, as said below
- orient: int32 [6, 16384], P(None, ('curve', 'sub')), may hold values from 0 to 7, as said below
Outputs:
- advanced: float32 [16384, 5, 512], P(('curve', 'sub'))
The draws below stay inside these ranges and needn't reach their ends.
Inputs may be any that keep to these rules, and one draw needn't show every extreme that they name: state_old has density and pressure between 0.5 and 2 at every node and velocity components within 1.2 in size; energy = pressure / 0.4 + 0.5 momenta . velocity. Every element index appears exactly once; on each device the live rows come first and hold consecutive element indices, the rest are -1; an element moves to its own device, the next or the previous one along curve+sub (device new_position // 128, row new_position % 128); a device sends at most 64 elements to each neighbour, and exactly 64 in every draw from some device to its next and from some device to its previous. partner[f, e] is the new index of the element sharing face f of element e, whose matching face is f xor 1, or -1 at a wall (only on -z and +z faces); matching is symmetric. A partner lies on the same device, or for a -z face of one of the first 16 rows of a device among the last 16 rows of the previous device, or for a +z face of one of the last 16 rows among the first 16 rows of the next device, along curve+sub. `orient`: the two sides of a shared face carry mutually inverse codes; at a wall the code is arbitrary.
All inputs are finite; a program needn't handle non-finite values.
Results may differ from the reference program's by a relative error of at most 0.0003.
Values sent between devices are 32-bit elements; how exact they have to be, the bound alone decides.
A program may use at most 128 MiB of HBM per device.

```python
import math
import jax
import jax.numpy as jnp
import numpy as np
from jax import lax

POINTS = 8
SIDE = 4
E_DEV = 128
NODES = 512
CAP_OLD = 256
TOTAL = 16384
OLD_TOTAL = 32768
DEVICES = 128


GAMMA = 1.4


def draw_state_old(key, part):
    base_key = jax.random.fold_in(key, 31)
    key_density, key_velocity, key_pressure = jax.random.split(base_key, 3)
    shape_nodes = (OLD_TOTAL, NODES)
    density = jax.random.uniform(key_density, shape_nodes, jnp.float32, 0.5, 2.0)
    velocity = jnp.clip(0.5 * jax.random.normal(key_velocity, (OLD_TOTAL, 3, NODES), jnp.float32), -1.2, 1.2)
    pressure = jax.random.uniform(key_pressure, shape_nodes, jnp.float32, 0.5, 2.0)
    momenta = density[:, None, :] * velocity
    energy = pressure / (GAMMA - 1.0) + 0.5 * jnp.sum(momenta * velocity, axis=1)
    return jnp.concatenate([density[:, None, :], momenta, energy[:, None, :]], axis=1)


def draw_new_position(key, part):
    base_key = jax.random.fold_in(key, 23)
    key_size, key_sign, key_pick = jax.random.split(base_key, 3)
    reach_rows = E_DEV // 2
    size_draw = jax.random.randint(key_size, (DEVICES - 1,), reach_rows // 4, reach_rows + 1, dtype=jnp.int32)
    sign_draw = 2 * jax.random.randint(key_sign, (DEVICES - 1,), 0, 2, dtype=jnp.int32) - 1
    inner_shift = size_draw * sign_draw
    picked = jax.random.permutation(key_pick, DEVICES - 1).astype(jnp.int32)
    inner_shift = inner_shift.at[picked[0]].set(reach_rows).at[picked[1]].set(-reach_rows)
    edge_zero = jnp.zeros((1,), jnp.int32)
    shifts = jnp.concatenate([edge_zero, inner_shift, edge_zero])
    device_ids = jnp.arange(DEVICES, dtype=jnp.int32)
    starts = device_ids * E_DEV + shifts[:-1]
    counts = E_DEV + shifts[1:] - shifts[:-1]
    row_ids = jnp.arange(CAP_OLD, dtype=jnp.int32)
    values = jnp.where(row_ids[None, :] < counts[:, None], starts[:, None] + row_ids[None, :], -1)
    return values.reshape(-1).astype(jnp.int32)


def shuffle_layer(key):
    return jax.random.permutation(key, SIDE * SIDE).astype(jnp.int32)


def inverse_code(codes):
    return jnp.where(codes < 4, codes, 4 + 2 * (codes % 2) + codes // 2 % 2)


def connectivity(key):
    base_key = jax.random.fold_in(key, 11)
    key_layers, key_codes = jax.random.split(base_key)
    depth = TOTAL // (SIDE * SIDE)
    shuffled = jax.vmap(shuffle_layer)(jax.random.split(key_layers, depth))
    stored = (jnp.arange(depth, dtype=jnp.int32)[:, None] * (SIDE * SIDE) + shuffled).reshape(depth, SIDE, SIDE)
    plus_codes = jax.random.randint(key_codes, (3, depth, SIDE, SIDE), 0, 8, dtype=jnp.int32)
    depth_pos = jnp.arange(depth, dtype=jnp.int32)[:, None, None]
    neighbors = [jnp.roll(stored, 1, axis=2), jnp.roll(stored, -1, axis=2), jnp.roll(stored, 1, axis=1), jnp.roll(stored, -1, axis=1), jnp.where(depth_pos == 0, -1, jnp.roll(stored, 1, axis=0)), jnp.where(depth_pos == depth - 1, -1, jnp.roll(stored, -1, axis=0))]
    codes = [inverse_code(jnp.roll(plus_codes[0], 1, axis=2)), plus_codes[0], inverse_code(jnp.roll(plus_codes[1], 1, axis=1)), plus_codes[1], inverse_code(jnp.roll(plus_codes[2], 1, axis=0)), plus_codes[2]]
    flat = stored.reshape(-1)
    partner_out = jnp.zeros((6, TOTAL), jnp.int32).at[:, flat].set(jnp.stack([item.reshape(-1) for item in neighbors]))
    orient_out = jnp.zeros((6, TOTAL), jnp.int32).at[:, flat].set(jnp.stack([item.reshape(-1) for item in codes]))
    return (partner_out, orient_out)


def draw_partner(key, part):
    return connectivity(key)[0]


def draw_orient(key, part):
    return connectivity(key)[1]


def block_scale(stream_key, dims, cuts, low, top_value):
    level, own = 1.0, jax.random.fold_in(stream_key, 6)
    for position, shards_of in cuts:
        steps = jnp.exp(jax.random.uniform(jax.random.fold_in(own, position), (shards_of,), jnp.float32, low / len(cuts), top_value / len(cuts)))
        level = level * jnp.repeat(steps, dims[position] // shards_of).reshape([-1 if axis == position else 1 for axis in range(len(dims))])
    return level


def setup_inputs(seed: int = 0) -> dict:
    keys = jax.random.split(jax.random.key(seed), 6)
    return {
        "state_old": draw_state_old(jax.random.fold_in(keys[5], 71), 0),
        "metric_old": jnp.clip(jnp.exp(math.log(4.0) - 1.3862944 * jax.random.uniform(keys[1], (OLD_TOTAL,), jnp.float32) ** block_scale(keys[1], (OLD_TOTAL,), ((0, 128),), -0.2, 0.2)), 1.0, 4.0),
        "new_position": draw_new_position(jax.random.fold_in(keys[5], 71), 0),
        "partner": draw_partner(jax.random.fold_in(keys[5], 71), 0),
        "orient": draw_orient(jax.random.fold_in(keys[5], 71), 0),
    }


GAMMA = 1.4
TIME_STEP = 0.002
FLIP_FACE = (1, 0, 3, 2, 5, 4)

def legendre_values(points, degree):
    previous = np.ones(points.shape)
    current = points.copy()
    for order_id in range(2, degree + 1):
        following = ((2 * order_id - 1) * points * current - (order_id - 1) * previous) / order_id
        previous = current
        current = following
    return (current, previous)

def lobatto_points(degree):
    points = np.cos(np.pi * np.arange(degree + 1) / degree)
    for sweep_id in range(100):
        current, previous = legendre_values(points, degree)
        points = points - (points * current - previous) / ((degree + 1) * current)
    points = points[::-1].copy()
    points[0] = -1.0
    points[degree] = 1.0
    return points

def node_tables(num_points):
    degree = num_points - 1
    points = lobatto_points(degree)
    values = legendre_values(points, degree)[0]
    weights = 2.0 / (degree * (degree + 1) * values ** 2)
    matrix = np.zeros((num_points, num_points))
    for row_pos in range(num_points):
        for col_pos in range(num_points):
            if row_pos != col_pos:
                matrix[row_pos, col_pos] = values[row_pos] / (values[col_pos] * (points[row_pos] - points[col_pos]))
    matrix[0, 0] = -degree * (degree + 1) / 4.0
    matrix[degree, degree] = degree * (degree + 1) / 4.0
    return (matrix, weights)

def kron_tables(matrix, num_points):
    single = np.eye(num_points)
    square = np.eye(num_points * num_points)
    along_x = np.kron(matrix, square)
    along_y = np.kron(single, np.kron(matrix, single))
    along_z = np.kron(square, matrix)
    return tuple((jnp.asarray(item.T, dtype=jnp.float32) for item in (along_x, along_y, along_z)))

def orient_tables(num_points):
    ordered = np.arange(num_points * num_points).reshape(num_points, num_points)
    tables = []
    for code_id in range(8):
        mapped = ordered.T if code_id >= 4 else ordered
        if code_id // 2 % 2:
            mapped = mapped[::-1, :]
        if code_id % 2:
            mapped = mapped[:, ::-1]
        tables.append(mapped.reshape(-1))
    return np.stack(tables)

def reflect_table():
    signs = np.ones((6, 5))
    for face_id in range(6):
        signs[face_id, 1 + face_id // 2] = -1.0
    return signs

def make_tables(num_points):
    matrix, weights = node_tables(num_points)
    return (kron_tables(matrix, num_points), jnp.asarray(orient_tables(num_points), dtype=jnp.int32), jnp.asarray(reflect_table(), dtype=jnp.float32), float(1.0 / weights[0]))

def primitives(fields):
    density = fields[..., 0, :]
    velocity = fields[..., 1:4, :] / density[..., None, :]
    kinetic = 0.5 * lax.optimization_barrier(jnp.sum(fields[..., 1:4, :] * velocity, axis=-2))
    pressure = (GAMMA - 1.0) * (fields[..., 4, :] - kinetic)
    return (velocity, pressure)

def axis_flux(fields, velocity, pressure, axis_dir):
    normal_vel = velocity[..., axis_dir, :]
    fluxes = fields * normal_vel[..., None, :]
    fluxes = fluxes.at[..., 1 + axis_dir, :].add(pressure)
    fluxes = fluxes.at[..., 4, :].add(pressure * normal_vel)
    return fluxes

def volume_term(fields, metric, kron_mats):
    velocity, pressure = primitives(fields)
    node_count = fields.shape[-1]
    total = jnp.zeros((fields.shape[0] * 5, node_count), jnp.float32)
    for axis_dir in range(3):
        fluxes = axis_flux(fields, velocity, pressure, axis_dir).reshape(-1, node_count)
        total = total + jnp.dot(fluxes, kron_mats[axis_dir], precision=lax.Precision.HIGHEST, preferred_element_type=jnp.float32)
    return -metric[:, None, None] * total.reshape(fields.shape)

def one_face(fields, face_id, num_points):
    cube_view = fields.reshape(fields.shape[:-1] + (num_points, num_points, num_points))
    edge_pos = 0 if face_id % 2 == 0 else num_points - 1
    sliced = lax.index_in_dim(cube_view, edge_pos, axis=2 + face_id // 2, keepdims=False)
    return sliced.reshape(fields.shape[:-1] + (num_points * num_points,))

def all_faces(fields, num_points):
    return jnp.stack([one_face(fields, face_id, num_points) for face_id in range(6)], axis=1)

def surface_term(inner_trace, outside, partners, orient_codes, metric, orient_perm, reflect, lift_gain):
    index_map = orient_perm[orient_codes]
    aligned = jnp.take_along_axis(outside, index_map[:, :, None, :], axis=3)
    walled = inner_trace * reflect[None, :, :, None]
    aligned = jnp.where(partners[:, :, None, None] >= 0, aligned, walled)
    vel_in, pres_in = primitives(inner_trace)
    vel_out, pres_out = primitives(aligned)
    sound_in = jnp.sqrt(GAMMA * pres_in / inner_trace[..., 0, :])
    sound_out = jnp.sqrt(GAMMA * pres_out / aligned[..., 0, :])
    pieces = []
    for face_id in range(6):
        axis_dir = face_id // 2
        sign_out = 1.0 if face_id % 2 else -1.0
        inner_face = inner_trace[:, face_id]
        outer_face = aligned[:, face_id]
        flux_in = sign_out * axis_flux(inner_face, vel_in[:, face_id], pres_in[:, face_id], axis_dir)
        flux_out = sign_out * axis_flux(outer_face, vel_out[:, face_id], pres_out[:, face_id], axis_dir)
        wave_speed = jnp.maximum(jnp.abs(vel_in[:, face_id, axis_dir]) + sound_in[:, face_id], jnp.abs(vel_out[:, face_id, axis_dir]) + sound_out[:, face_id])
        flux_jump = 0.5 * (flux_out - flux_in) - 0.5 * wave_speed[:, None, :] * (outer_face - inner_face)
        pieces.append(-(metric * lift_gain)[:, None, None] * flux_jump)
    return jnp.stack(pieces, axis=1)

def add_faces(residual, corrections, num_points):
    cube_view = residual.reshape(residual.shape[:-1] + (num_points, num_points, num_points))
    face_shape = residual.shape[:-1] + (num_points, num_points)
    last_pos = num_points - 1
    cube_view = cube_view.at[:, :, 0].add(corrections[:, 0].reshape(face_shape))
    cube_view = cube_view.at[:, :, last_pos].add(corrections[:, 1].reshape(face_shape))
    cube_view = cube_view.at[:, :, :, 0].add(corrections[:, 2].reshape(face_shape))
    cube_view = cube_view.at[:, :, :, last_pos].add(corrections[:, 3].reshape(face_shape))
    cube_view = cube_view.at[:, :, :, :, 0].add(corrections[:, 4].reshape(face_shape))
    cube_view = cube_view.at[:, :, :, :, last_pos].add(corrections[:, 5].reshape(face_shape))
    return cube_view.reshape(residual.shape)

def section_update(fields, metric, volume, inner_trace, outside, partners, orient_codes, tables, num_points):
    corrections = surface_term(inner_trace, outside, partners, orient_codes, metric, tables[1], tables[2], tables[3])
    residual = add_faces(volume, corrections, num_points)
    return fields + TIME_STEP * residual

def reference(state_old, metric_old, new_position, partner, orient):
    tables = make_tables(POINTS)
    target_index = jnp.where(new_position >= 0, new_position, TOTAL).astype(jnp.int32)
    placed = jnp.zeros((TOTAL,) + state_old.shape[1:], jnp.float32).at[target_index].set(state_old, mode='drop')
    metric_new = jnp.zeros((TOTAL,), jnp.float32).at[target_index].set(metric_old, mode='drop')
    blocks = TOTAL // E_DEV

    def one_block(block_id):
        first_row = (block_id * E_DEV).astype(jnp.int32)
        fields = lax.dynamic_slice_in_dim(placed, first_row, E_DEV, 0)
        metric = lax.dynamic_slice_in_dim(metric_new, first_row, E_DEV, 0)
        partners = lax.dynamic_slice_in_dim(partner, first_row, E_DEV, 1).T
        orient_codes = lax.dynamic_slice_in_dim(orient, first_row, E_DEV, 1).T
        inner_trace = all_faces(fields, POINTS)
        outside = jnp.stack([one_face(placed[jnp.maximum(partners[:, face_id], 0)], FLIP_FACE[face_id], POINTS) for face_id in range(6)], axis=1)
        volume = volume_term(fields, metric, tables[0])
        return section_update(fields, metric, volume, inner_trace, outside, partners, orient_codes, tables, POINTS)
    result = lax.map(one_block, jnp.arange(blocks, dtype=jnp.int32))
    return result.reshape((TOTAL,) + state_old.shape[1:])
```

```python
import functools

import jax
import jax.numpy as jnp
import numpy as np
from jax import lax
from jax.experimental import pallas as pl
from jax.experimental.pallas import tpu as pltpu
from jax.sharding import PartitionSpec as P

POINTS = 8
RIM = 16
VARS = 5
GAMMA = 1.4
TIME_STEP = 0.002
MESH = pl.DeviceIdType.MESH
CHUNKS = 4
ORDER = (0, 3, 1, 2)
PAD = 320
VMEM_LIMIT = 64 * 1024 * 1024
LANES = 128


def legendre_values(points, degree):
    previous = np.ones(points.shape)
    current = points.copy()
    for order_id in range(2, degree + 1):
        following = ((2 * order_id - 1) * points * current - (order_id - 1) * previous) / order_id
        previous = current
        current = following
    return (current, previous)


def lobatto_points(degree):
    points = np.cos(np.pi * np.arange(degree + 1) / degree)
    for sweep_id in range(100):
        current, previous = legendre_values(points, degree)
        points = points - (points * current - previous) / ((degree + 1) * current)
    points = points[::-1].copy()
    points[0] = -1.0
    points[degree] = 1.0
    return points


def node_tables(num_points):
    degree = num_points - 1
    points = lobatto_points(degree)
    values = legendre_values(points, degree)[0]
    weights = 2.0 / (degree * (degree + 1) * values**2)
    matrix = np.zeros((num_points, num_points))
    for row_pos in range(num_points):
        for col_pos in range(num_points):
            if row_pos != col_pos:
                matrix[row_pos, col_pos] = values[row_pos] / (
                    values[col_pos] * (points[row_pos] - points[col_pos])
                )
    matrix[0, 0] = -degree * (degree + 1) / 4.0
    matrix[degree, degree] = degree * (degree + 1) / 4.0
    return (matrix, weights)


def derivative(matrix, values):
    evens = [values[place] + values[7 - place] for place in range(4)]
    odds = [values[place] - values[7 - place] for place in range(4)]
    first, second = [], []
    for row in range(4):
        even, odd = [
            functools.reduce(
                lambda left, right: left + right,
                [
                    float(0.5 * (matrix[row, col] + sign * matrix[row, 7 - col])) * items[col]
                    for col in range(4)
                ],
            )
            for sign, items in ((1.0, evens), (-1.0, odds))
        ]
        first.append(even + odd)
        second.append(odd - even)
    return first + second[::-1]


def pick(values, index, axis):
    other = 1 - axis
    numbers = lax.GatherDimensionNumbers(
        offset_dims=(),
        collapsed_slice_dims=(axis,),
        start_index_map=(axis,),
        operand_batching_dims=(other,),
        start_indices_batching_dims=(other,),
    )
    return lax.gather(
        values, index[..., None], numbers, (1, 1), mode=lax.GatherScatterMode.PROMISE_IN_BOUNDS
    )


def trace_rows(face_id, layer):
    edge = 0 if face_id % 2 == 0 else POINTS - 1
    return ((edge * 64 + layer * 8, 1), (layer * 64 + edge * 8, 1), (layer * 64 + edge, 8))[face_id // 2]


def at_rows(rows):
    first, stride = rows
    return pl.ds(first, 8) if stride == 1 else pl.ds(first, 8, stride=stride)


def side_terms(state, axis_dir):
    density, energy = state[0], state[4]
    inverse = 1.0 / density
    momenta = state[1:4]
    kinetic = 0.5 * inverse * (momenta[0] * momenta[0] + momenta[1] * momenta[1] + momenta[2] * momenta[2])
    pressure = (GAMMA - 1.0) * (energy - kinetic)
    normal = momenta[axis_dir] * inverse
    speed = jnp.abs(normal) + jnp.sqrt(GAMMA * pressure * inverse)
    flux = [momenta[axis_dir]] + [item * normal for item in momenta] + [(energy + pressure) * normal]
    flux[1 + axis_dir] = flux[1 + axis_dir] + pressure
    return flux, speed


def kernel(
    matrix,
    lift,
    position_row_hbm,
    position_hbm,
    metric_hbm,
    partner_hbm,
    orient_hbm,
    state_hbm,
    result,
    first_ref,
    position_ref,
    metric_ref,
    partner_ref,
    orient_ref,
    staged_0,
    staged_1,
    staged_2,
    staged_3,
    send,
    recv,
    rim_send,
    rim_recv,
    rim_own,
    rim_turned,
    nodal,
    total,
    flux_x,
    flux_y,
    flux_z,
    slope_z,
    fetched,
    in_sem,
    table_sem,
    send_sem,
    recv_sem,
    rim_send_sem,
    rim_recv_sem,
):
    sub_size = lax.axis_size("sub")
    devices = lax.axis_size("curve") * sub_size
    me = lax.axis_index("curve") * sub_size + lax.axis_index("sub")
    has_next, has_prev = me < devices - 1, me > 0
    after, before = jnp.minimum(me + 1, devices - 1), jnp.maximum(me - 1, 0)
    sides = ((after // sub_size, lax.rem(after, sub_size)), (before // sub_size, lax.rem(before, sub_size)))
    sent, arrives = (has_next, has_prev), (has_prev, has_next)

    barrier = pltpu.get_barrier_semaphore()
    for way in range(2):

        @pl.when(sent[way])
        def _():
            pl.semaphore_signal(barrier, inc=1, device_id=sides[way], device_id_type=MESH)

    tables = [
        pltpu.make_async_copy(source, target, table_sem.at[place])
        for place, (source, target) in enumerate(
            (
                (position_row_hbm, first_ref),
                (position_hbm, position_ref),
                (metric_hbm, metric_ref),
                (partner_hbm, partner_ref),
                (orient_hbm, orient_ref),
            )
        )
    ]
    for copy in tables[:2]:
        copy.start()
    staged = (staged_0, staged_1, staged_2, staged_3)
    loads = [
        pltpu.make_async_copy(
            state_hbm.at[:, :, pl.ds(chunk * LANES, LANES)],
            staged[chunk].at[:, pl.ds(PAD, 256), :],
            in_sem.at[chunk],
        )
        for chunk in range(CHUNKS)
    ]
    for chunk in ORDER:
        loads[chunk].start()
    for copy in tables[2:]:
        copy.start()
    for copy in tables[:2]:
        copy.wait()

    shift = me * LANES - first_ref[0]
    start = PAD + jnp.clip(shift, -255, 128)
    alive = jnp.where(position_ref[...] >= 0, 1.0, 0.0)
    count = jnp.sum(alive).astype(jnp.int32)
    low, high = -shift, count - shift

    def rows_at(chunk, var, local, size):
        block = staged[chunk][var, pl.ds(start + local, size), :]
        row = local + lax.broadcasted_iota(jnp.int32, (size, LANES), 0)
        return jnp.where((row >= low) & (row < high), block, 0.0)

    def to_side(source, target, send_sems, recv_sems, way):
        return pltpu.make_async_remote_copy(
            src_ref=source,
            dst_ref=target,
            send_sem=send_sems,
            recv_sem=recv_sems,
            device_id=sides[way],
            device_id_type=MESH,
        )

    def start_if(way, copy):
        @pl.when(sent[way])
        def _():
            copy.start()

    def finish(way, copy, target):
        @pl.when(sent[way])
        def _():
            copy.wait_send()

        @pl.when(arrives[way])
        def _():
            copy.wait_recv()

        @pl.when(jnp.logical_not(arrives[way]))
        def _():
            target[...] = jnp.zeros(target.shape, jnp.float32)

    def chunk_copy(way, chunk):
        return to_side(
            send.at[way, chunk], recv.at[way, chunk], send_sem.at[way, chunk], recv_sem.at[way, chunk], way
        )

    def rim_copy(way):
        return to_side(rim_send.at[way], rim_recv.at[way], rim_send_sem.at[way], rim_recv_sem.at[way], way)

    def send_chunk(chunk):
        for way in range(2):
            start_if(way, chunk_copy(way, chunk))

    for step, chunk in enumerate(ORDER):
        loads[chunk].wait()
        for way, local in ((0, LANES), (1, -64)):
            for var in range(VARS):
                send[way, chunk, var] = rows_at(chunk, var, local, 64)
        if step == 0:
            pl.semaphore_wait(barrier, has_next.astype(jnp.int32) + has_prev.astype(jnp.int32))

        if step < CHUNKS - 1:
            send_chunk(chunk)
    for copy in tables[2:]:
        copy.wait()

    lane = lax.broadcasted_iota(jnp.int32, (RIM, LANES), 1)
    upper = lane >= 64
    spot = lax.rem(lane, 16) * 8 + jnp.where(upper, 0, POINTS - 1)
    piece = lax.rem(lane, 64) // 16
    for var in range(VARS):
        zero = jnp.zeros((RIM, LANES), jnp.float32)
        to_next, to_prev, own_below, own_above = zero, zero, zero, zero
        for chunk in range(CHUNKS):
            here = piece == chunk
            to_next = jnp.where(here, pick(rows_at(chunk, var, LANES - RIM, RIM), spot, 1), to_next)
            to_prev = jnp.where(here, pick(rows_at(chunk, var, 0, RIM), spot, 1), to_prev)
            own_below = jnp.where(here, pick(rows_at(chunk, var, -RIM, RIM), spot, 1), own_below)
            own_above = jnp.where(here, pick(rows_at(chunk, var, LANES, RIM), spot, 1), own_above)
        place = pl.ds(var * RIM, RIM)
        rim_send[0, place, :] = jnp.where(upper, 0.0, to_next)
        rim_send[1, place, :] = jnp.where(upper, to_prev, 0.0)
        rim_own[place, :] = jnp.where(upper, own_above, own_below)

    lane8 = lax.broadcasted_iota(jnp.int32, (8, LANES), 1)
    halves = [jnp.broadcast_to(metric_ref[pl.ds(half, 1), :], (8, LANES)) for half in range(2)]

    def scale_at(local):
        row = local + lane8
        index = row + shift
        value = jnp.where(index < LANES, pick(halves[0], index & 127, 1), pick(halves[1], index & 127, 1))
        return jnp.where((row >= low) & (row < high), value, 0.0)

    last = pl.ds(VARS * RIM, 8)
    rim_send[0, last, :] = jnp.where(lane8 < 64, scale_at(LANES), 0.0)
    rim_send[1, last, :] = jnp.where(lane8 >= 64, scale_at(-LANES), 0.0)
    rim_own[last, :] = scale_at(0)
    for way in range(2):
        start_if(way, rim_copy(way))
    send_chunk(ORDER[-1])

    def absorb(chunk, first):
        for way in range(2):
            finish(way, chunk_copy(way, chunk), recv.at[way, chunk])
        for var in range(VARS):
            moved = jnp.concatenate([recv[0, chunk, var], recv[1, chunk, var]], axis=0)
            nodal[var, pl.ds(chunk * LANES, LANES), :] = (rows_at(chunk, var, 0, LANES) + moved).T
        for part in range(8):
            rows = pl.ds(chunk * LANES + part * 16, 16)
            state = [nodal[var, rows, :] for var in range(VARS)]
            inverse = 1.0 / state[0]
            velocity = [item * inverse for item in state[1:4]]
            kinetic = 0.5 * (state[1] * velocity[0] + state[2] * velocity[1] + state[3] * velocity[2])
            pressure = (GAMMA - 1.0) * (state[4] - kinetic)
            enthalpy = state[4] + pressure
            for axis_dir, target in enumerate((flux_x, flux_y, flux_z)):
                flux = [state[1 + axis_dir]]
                for other in range(3):
                    product = state[1 + other] * velocity[axis_dir]
                    flux.append(product + pressure if other == axis_dir else product)
                flux.append(enthalpy * velocity[axis_dir])
                for var in range(VARS):
                    target[var, rows, :] = flux[var]
        layers = (2 * chunk, 2 * chunk + 1)
        for var in range(VARS):
            for layer in layers:
                base = layer * 64
                rows = [pl.ds(base + place, 8, stride=8) for place in range(8)]
                parts = derivative(matrix, [flux_z[var, rows[place], :] for place in range(8)])
                for place in range(8):
                    slope_z[var, rows[place], :] = parts[place]
            along_y = [
                derivative(matrix, [flux_y[var, pl.ds(layer * 64 + 8 * place, 8), :] for place in range(8)])
                for layer in layers
            ]
            for group in range(8):
                values = [flux_x[var, pl.ds(layer * 64 + 8 * group, 8), :] for layer in layers]
                for target in range(8):
                    rows = pl.ds(target * 64 + 8 * group, 8)
                    value = float(matrix[target, layers[0]]) * values[0]
                    value = value + float(matrix[target, layers[1]]) * values[1]
                    if target in layers:
                        value = value + along_y[target - layers[0]][group] + slope_z[var, rows, :]
                    total[var, rows, :] = value if first else total[var, rows, :] + value

    def across(face_id):
        partner = jnp.broadcast_to(partner_ref[pl.ds(face_id, 1), :], (8, LANES))
        return partner, partner & 127

    def fetch_layers(face_ids, layers):
        for face_id in face_ids:
            partner, local = across(face_id)
            away = (partner >> 7) != me
            for layer in layers:
                for var in range(VARS):
                    value = pick(nodal[var, at_rows(trace_rows(face_id ^ 1, layer)), :], local, 1)
                    if face_id >= 4:
                        base = 0 if face_id == 4 else 64
                        index = (partner & (RIM - 1)) + var * RIM
                        other = pick(rim_turned[pl.ds(base + layer * 8, 8), :], index, 1)
                        value = jnp.where(away, other, value)
                    fetched[face_id, var, pl.ds(layer * 8, 8), :] = value

    row8 = lax.broadcasted_iota(jnp.int32, (8, LANES), 0)

    def correct(face_id):
        axis_dir, sign_out = face_id // 2, 1.0 if face_id % 2 else -1.0
        partner, _ = across(face_id)
        code = jnp.broadcast_to(orient_ref[pl.ds(face_id, 1), :], (8, LANES))
        turned = code >= 4
        flip_first = (code & 2) != 0
        flip_second = jnp.where((code & 1) != 0, 7 - row8, row8)
        wall = partner < 0
        for layer in range(4):
            pair = (layer, 7 - layer)
            aligned = [[], []]
            for var in range(VARS):
                near, far = [
                    jnp.where(
                        turned,
                        fetched[face_id, var, pl.ds(place, 8, stride=8), :],
                        fetched[face_id, var, pl.ds(place * 8, 8), :],
                    )
                    for place in pair
                ]
                aligned[0].append(pick(jnp.where(flip_first, far, near), flip_second, 0))
                aligned[1].append(pick(jnp.where(flip_first, near, far), flip_second, 0))
            for which in range(2):
                rows = at_rows(trace_rows(face_id, pair[which]))
                inner = [nodal[var, rows, :] for var in range(VARS)]
                outer = aligned[which]
                if axis_dir == 2:
                    outer = [
                        jnp.where(wall, -inner[var] if var == 1 + axis_dir else inner[var], outer[var])
                        for var in range(VARS)
                    ]
                flux_in, speed_in = side_terms(inner, axis_dir)
                flux_out, speed_out = side_terms(outer, axis_dir)
                wave = jnp.maximum(speed_in, speed_out)
                for var in range(VARS):
                    jump = sign_out * (flux_out[var] - flux_in[var]) - wave * (outer[var] - inner[var])
                    total[var, rows, :] = total[var, rows, :] + (0.5 * lift) * jump

    def layers_of(chunks):
        return [layer for chunk in chunks for layer in (2 * chunk, 2 * chunk + 1)]

    absorb(ORDER[0], True)
    absorb(ORDER[1], False)
    fetch_layers((0, 1), range(8))
    correct(0)
    correct(1)
    absorb(ORDER[2], False)
    fetch_layers((2, 3), layers_of(ORDER[:3]))
    for way in range(2):
        finish(way, rim_copy(way), rim_recv.at[way])
    rim = rim_own[...] + rim_recv[0] + rim_recv[1]
    scale = rim[VARS * RIM :, :]
    padded = jnp.concatenate([rim[: VARS * RIM], jnp.zeros((LANES - VARS * RIM, LANES), jnp.float32)], axis=0)
    rim_turned[...] = padded.T
    fetch_layers((4, 5), layers_of(ORDER[:3]))
    absorb(ORDER[3], False)
    fetch_layers((2, 3, 4, 5), layers_of(ORDER[3:]))
    for face_id in range(2, 6):
        correct(face_id)

    factor = jnp.broadcast_to((-TIME_STEP) * scale[:1, :], (LANES, LANES))
    for var in range(VARS):
        for chunk in range(CHUNKS):
            rows = pl.ds(chunk * LANES, LANES)
            result[var, :, rows] = (nodal[var, rows, :] + factor * total[var, rows, :]).T


def body(state_old, metric_old, new_position, partner, orient):
    matrix, weights = node_tables(POINTS)
    nodes = state_old.shape[2]
    rows_dev = partner.shape[1]
    cube = pltpu.VMEM((VARS, nodes, LANES), jnp.float32)
    advanced = pl.pallas_call(
        functools.partial(kernel, matrix, float(1.0 / weights[0])),
        out_shape=jax.ShapeDtypeStruct((VARS, rows_dev, nodes), jnp.float32),
        in_specs=[pl.BlockSpec(memory_space=pltpu.HBM)] * 6,
        out_specs=pl.BlockSpec(memory_space=pltpu.VMEM),
        scratch_shapes=[
            pltpu.SMEM((256,), jnp.int32),
            pltpu.VMEM((2, LANES), jnp.int32),
            pltpu.VMEM((2, LANES), jnp.float32),
            pltpu.VMEM((6, LANES), jnp.int32),
            pltpu.VMEM((6, LANES), jnp.int32),
        ]
        + [pltpu.VMEM((VARS, 2 * PAD, LANES), jnp.float32)] * CHUNKS
        + [
            pltpu.VMEM((2, CHUNKS, VARS, 64, LANES), jnp.float32),
            pltpu.VMEM((2, CHUNKS, VARS, 64, LANES), jnp.float32),
            pltpu.VMEM((2, VARS * RIM + 8, LANES), jnp.float32),
            pltpu.VMEM((2, VARS * RIM + 8, LANES), jnp.float32),
            pltpu.VMEM((VARS * RIM + 8, LANES), jnp.float32),
            pltpu.VMEM((LANES, LANES), jnp.float32),
        ]
        + [cube] * 6
        + [
            pltpu.VMEM((6, VARS, 64, LANES), jnp.float32),
            pltpu.SemaphoreType.DMA((CHUNKS,)),
            pltpu.SemaphoreType.DMA((5,)),
            pltpu.SemaphoreType.DMA((2, CHUNKS)),
            pltpu.SemaphoreType.DMA((2, CHUNKS)),
            pltpu.SemaphoreType.DMA((2,)),
            pltpu.SemaphoreType.DMA((2,)),
        ],
        compiler_params=pltpu.CompilerParams(
            collective_id=0, has_side_effects=True, vmem_limit_bytes=VMEM_LIMIT
        ),
    )(
        new_position,
        new_position.reshape(2, LANES),
        metric_old.reshape(2, LANES),
        partner,
        orient,
        state_old.transpose(1, 0, 2),
    )
    return advanced.transpose(1, 0, 2)


def solution(mesh):
    placed = (
        P(("curve", "sub"), None, None),
        P(("curve", "sub")),
        P(("curve", "sub")),
        P(None, ("curve", "sub")),
        P(None, ("curve", "sub")),
    )
    return jax.shard_map(
        body, mesh=mesh, in_specs=placed, out_specs=P(("curve", "sub"), None, None), check_vma=False
    )
```

```python
import functools

import jax
import jax.numpy as jnp
import numpy as np
from jax import lax
from jax.experimental import pallas as pl
from jax.experimental.pallas import tpu as pltpu
from jax.sharding import PartitionSpec as P

POINTS = 8
RIM = 16
VARS = 5
GAMMA = 1.4
TIME_STEP = 0.002
MESH = pl.DeviceIdType.MESH
CHUNKS = 4
ORDER = (0, 3, 1, 2)
PAD = 320
VMEM_LIMIT = 50 * 1024 * 1024
LANES = 128


def legendre_values(points, degree):
    previous = np.ones(points.shape)
    current = points.copy()
    for order_id in range(2, degree + 1):
        following = ((2 * order_id - 1) * points * current - (order_id - 1) * previous) / order_id
        previous = current
        current = following
    return (current, previous)


def lobatto_points(degree):
    points = np.cos(np.pi * np.arange(degree + 1) / degree)
    for sweep_id in range(100):
        current, previous = legendre_values(points, degree)
        points = points - (points * current - previous) / ((degree + 1) * current)
    points = points[::-1].copy()
    points[0] = -1.0
    points[degree] = 1.0
    return points


def node_tables(num_points):
    degree = num_points - 1
    points = lobatto_points(degree)
    values = legendre_values(points, degree)[0]
    weights = 2.0 / (degree * (degree + 1) * values**2)
    matrix = np.zeros((num_points, num_points))
    for row_pos in range(num_points):
        for col_pos in range(num_points):
            if row_pos != col_pos:
                matrix[row_pos, col_pos] = values[row_pos] / (
                    values[col_pos] * (points[row_pos] - points[col_pos])
                )
    matrix[0, 0] = -degree * (degree + 1) / 4.0
    matrix[degree, degree] = degree * (degree + 1) / 4.0
    return (matrix, weights)


def derivative(matrix, values):
    evens = [values[place] + values[7 - place] for place in range(4)]
    odds = [values[place] - values[7 - place] for place in range(4)]
    first, second = [], []
    for row in range(4):
        even, odd = [
            functools.reduce(
                lambda left, right: left + right,
                [
                    float(0.5 * (matrix[row, col] + sign * matrix[row, 7 - col])) * items[col]
                    for col in range(4)
                ],
            )
            for sign, items in ((1.0, evens), (-1.0, odds))
        ]
        first.append(even + odd)
        second.append(odd - even)
    return first + second[::-1]


def pick(values, index, axis):
    other = 1 - axis
    numbers = lax.GatherDimensionNumbers(
        offset_dims=(),
        collapsed_slice_dims=(axis,),
        start_index_map=(axis,),
        operand_batching_dims=(other,),
        start_indices_batching_dims=(other,),
    )
    return lax.gather(
        values, index[..., None], numbers, (1, 1), mode=lax.GatherScatterMode.PROMISE_IN_BOUNDS
    )


def trace_rows(face_id, layer):
    edge = 0 if face_id % 2 == 0 else POINTS - 1
    return ((edge * 64 + layer * 8, 1), (layer * 64 + edge * 8, 1), (layer * 64 + edge, 8))[face_id // 2]


def at_rows(rows):
    first, stride = rows
    return pl.ds(first, 8) if stride == 1 else pl.ds(first, 8, stride=stride)


def side_terms(state, axis_dir):
    density, energy = state[0], state[4]
    inverse = 1.0 / density
    momenta = state[1:4]
    kinetic = 0.5 * inverse * (momenta[0] * momenta[0] + momenta[1] * momenta[1] + momenta[2] * momenta[2])
    pressure = (GAMMA - 1.0) * (energy - kinetic)
    normal = momenta[axis_dir] * inverse
    speed = jnp.abs(normal) + jnp.sqrt(GAMMA * pressure * inverse)
    flux = [momenta[axis_dir]] + [item * normal for item in momenta] + [(energy + pressure) * normal]
    flux[1 + axis_dir] = flux[1 + axis_dir] + pressure
    return flux, speed


def kernel(
    matrix,
    lift,
    position_row_hbm,
    position_hbm,
    metric_hbm,
    partner_hbm,
    orient_hbm,
    state_hbm,
    result,
    first_ref,
    position_ref,
    metric_ref,
    partner_ref,
    orient_ref,
    staged_0,
    staged_1,
    staged_2,
    staged_3,
    send,
    recv,
    rim_send,
    rim_recv,
    rim_own,
    rim_turned,
    nodal,
    total,
    flux_x,
    flux_y,
    flux_z,
    slope_z,
    fetched,
    in_sem,
    table_sem,
    send_sem,
    recv_sem,
    rim_send_sem,
    rim_recv_sem,
):
    sub_size = lax.axis_size("sub")
    devices = lax.axis_size("curve") * sub_size
    me = lax.axis_index("curve") * sub_size + lax.axis_index("sub")
    has_next, has_prev = me < devices - 1, me > 0
    after, before = jnp.minimum(me + 1, devices - 1), jnp.maximum(me - 1, 0)
    sides = ((after // sub_size, lax.rem(after, sub_size)), (before // sub_size, lax.rem(before, sub_size)))
    sent, arrives = (has_next, has_prev), (has_prev, has_next)

    barrier = pltpu.get_barrier_semaphore()
    for way in range(2):

        @pl.when(sent[way])
        def _():
            pl.semaphore_signal(barrier, inc=1, device_id=sides[way], device_id_type=MESH)

    tables = [
        pltpu.make_async_copy(source, target, table_sem.at[place])
        for place, (source, target) in enumerate(
            (
                (position_row_hbm, first_ref),
                (position_hbm, position_ref),
                (metric_hbm, metric_ref),
                (partner_hbm, partner_ref),
                (orient_hbm, orient_ref),
            )
        )
    ]
    for copy in tables[:2]:
        copy.start()
    staged = (staged_0, staged_1, staged_2, staged_3)
    loads = [
        pltpu.make_async_copy(
            state_hbm.at[:, :, pl.ds(chunk * LANES, LANES)],
            staged[chunk].at[:, pl.ds(PAD, 256), :],
            in_sem.at[chunk],
        )
        for chunk in range(CHUNKS)
    ]
    for chunk in ORDER:
        loads[chunk].start()
    for copy in tables[2:]:
        copy.start()
    for copy in tables[:2]:
        copy.wait()

    shift = me * LANES - first_ref[0]
    start = PAD + jnp.clip(shift, -255, 128)
    alive = jnp.where(position_ref[...] >= 0, 1.0, 0.0)
    count = jnp.sum(alive).astype(jnp.int32)
    low, high = -shift, count - shift

    def rows_at(chunk, var, local, size):
        block = staged[chunk][var, pl.ds(start + local, size), :]
        row = local + lax.broadcasted_iota(jnp.int32, (size, LANES), 0)
        return jnp.where((row >= low) & (row < high), block, 0.0)

    def to_side(source, target, send_sems, recv_sems, way):
        return pltpu.make_async_remote_copy(
            src_ref=source,
            dst_ref=target,
            send_sem=send_sems,
            recv_sem=recv_sems,
            device_id=sides[way],
            device_id_type=MESH,
        )

    def start_if(way, copy):
        @pl.when(sent[way])
        def _():
            copy.start()

    def finish(way, copy, target):
        @pl.when(arrives[way])
        def _():
            copy.wait_recv()

        @pl.when(jnp.logical_not(arrives[way]))
        def _():
            target[...] = jnp.zeros(target.shape, jnp.float32)

    def chunk_copy(way, chunk):
        return to_side(
            send.at[way, chunk], recv.at[way, chunk], send_sem.at[way, chunk], recv_sem.at[way, chunk], way
        )

    def rim_copy(way):
        return to_side(rim_send.at[way], rim_recv.at[way], rim_send_sem.at[way], rim_recv_sem.at[way], way)

    def send_chunk(chunk):
        for way in range(2):
            start_if(way, chunk_copy(way, chunk))

    for step, chunk in enumerate(ORDER):
        loads[chunk].wait()
        for way, local in ((0, LANES), (1, -64)):
            for var in range(VARS):
                send[way, chunk, var] = rows_at(chunk, var, local, 64)
        if step == 0:
            pl.semaphore_wait(barrier, has_next.astype(jnp.int32) + has_prev.astype(jnp.int32))
        if step < CHUNKS - 1:
            send_chunk(chunk)
    for copy in tables[2:]:
        copy.wait()

    lane8 = lax.broadcasted_iota(jnp.int32, (8, LANES), 1)
    upper = lane8 >= 64
    piece = lax.rem(lane8, 64) // 16
    bottom = lax.rem(lane8, 16) * 8
    top = bottom + POINTS - 1
    for target, local, spot in (
        (rim_send.at[0], LANES - RIM, top),
        (rim_send.at[1], 0, bottom),
        (rim_own.at[0], -RIM, top),
        (rim_own.at[1], LANES, bottom),
    ):
        for var in range(VARS):
            value = None
            for chunk in range(CHUNKS):
                rows = rows_at(chunk, var, local, RIM)
                part = jnp.where(upper, pick(rows[8:], spot, 1), pick(rows[:8], spot, 1))
                value = part if value is None else jnp.where(piece == chunk, part, value)
            target[pl.ds(var * 8, 8), :] = value

    halves = [jnp.broadcast_to(metric_ref[pl.ds(half, 1), :], (8, LANES)) for half in range(2)]

    def scale_at(local):
        row = local + lane8
        index = row + shift
        value = jnp.where(index < LANES, pick(halves[0], index & 127, 1), pick(halves[1], index & 127, 1))
        return jnp.where((row >= low) & (row < high), value, 0.0)

    last = pl.ds(VARS * 8, 8)
    rim_send[0, last, :] = jnp.where(upper, 0.0, scale_at(LANES))
    rim_send[1, last, :] = jnp.where(upper, scale_at(-LANES), 0.0)

    for way in range(2):
        start_if(way, rim_copy(way))
    send_chunk(ORDER[-1])

    def absorb(chunk, first):
        for way in range(2):
            finish(way, chunk_copy(way, chunk), recv.at[way, chunk])
        for var in range(VARS):
            moved = jnp.concatenate([recv[0, chunk, var], recv[1, chunk, var]], axis=0)
            nodal[var, pl.ds(chunk * LANES, LANES), :] = (rows_at(chunk, var, 0, LANES) + moved).T
        for part in range(8):
            rows = pl.ds(chunk * LANES + part * 16, 16)
            state = [nodal[var, rows, :] for var in range(VARS)]
            inverse = 1.0 / state[0]
            velocity = [item * inverse for item in state[1:4]]
            kinetic = 0.5 * (state[1] * velocity[0] + state[2] * velocity[1] + state[3] * velocity[2])
            pressure = (GAMMA - 1.0) * (state[4] - kinetic)
            enthalpy = state[4] + pressure
            for axis_dir, target in enumerate((flux_x, flux_y, flux_z)):
                flux = [state[1 + axis_dir]]
                for other in range(3):
                    product = state[1 + other] * velocity[axis_dir]
                    flux.append(product + pressure if other == axis_dir else product)
                flux.append(enthalpy * velocity[axis_dir])
                for var in range(VARS):
                    target[var, rows, :] = flux[var]
        layers = (2 * chunk, 2 * chunk + 1)
        for var in range(VARS):
            for layer in layers:
                base = layer * 64
                rows = [pl.ds(base + place, 8, stride=8) for place in range(8)]
                parts = derivative(matrix, [flux_z[var, rows[place], :] for place in range(8)])
                for place in range(8):
                    slope_z[var, rows[place], :] = parts[place]
            along_y = [
                derivative(matrix, [flux_y[var, pl.ds(layer * 64 + 8 * place, 8), :] for place in range(8)])
                for layer in layers
            ]
            for group in range(8):
                values = [flux_x[var, pl.ds(layer * 64 + 8 * group, 8), :] for layer in layers]
                for target in range(8):
                    rows = pl.ds(target * 64 + 8 * group, 8)
                    value = float(matrix[target, layers[0]]) * values[0]
                    value = value + float(matrix[target, layers[1]]) * values[1]
                    if target in layers:
                        value = value + along_y[target - layers[0]][group] + slope_z[var, rows, :]
                    total[var, rows, :] = value if first else total[var, rows, :] + value

    def across(face_id):
        partner = jnp.broadcast_to(partner_ref[pl.ds(face_id, 1), :], (8, LANES))
        return partner, partner & 127

    def fetch_layers(face_ids, layers):
        for face_id in face_ids:
            partner, local = across(face_id)
            away = (partner >> 7) != me
            for layer in layers:
                for var in range(VARS):
                    value = pick(nodal[var, at_rows(trace_rows(face_id ^ 1, layer)), :], local, 1)
                    if face_id >= 4:
                        index = (partner & 7) + var * 8 + (0 if face_id == 4 else 64)
                        other = jnp.where(
                            (partner & 8) == 0,
                            pick(rim_turned[pl.ds(layer * 8, 8), :], index, 1),
                            pick(rim_turned[pl.ds(64 + layer * 8, 8), :], index, 1),
                        )
                        value = jnp.where(away, other, value)
                    fetched[face_id, var, pl.ds(layer * 8, 8), :] = value

    row8 = lax.broadcasted_iota(jnp.int32, (8, LANES), 0)

    def correct(face_id):
        axis_dir, sign_out = face_id // 2, 1.0 if face_id % 2 else -1.0
        partner, _ = across(face_id)
        code = jnp.broadcast_to(orient_ref[pl.ds(face_id, 1), :], (8, LANES))
        turned = code >= 4
        flip_first = (code & 2) != 0
        flip_second = jnp.where((code & 1) != 0, 7 - row8, row8)
        wall = partner < 0
        for layer in range(4):
            pair = (layer, 7 - layer)
            aligned = [[], []]
            for var in range(VARS):
                near, far = [
                    jnp.where(
                        turned,
                        fetched[face_id, var, pl.ds(place, 8, stride=8), :],
                        fetched[face_id, var, pl.ds(place * 8, 8), :],
                    )
                    for place in pair
                ]
                aligned[0].append(pick(jnp.where(flip_first, far, near), flip_second, 0))
                aligned[1].append(pick(jnp.where(flip_first, near, far), flip_second, 0))
            for which in range(2):
                rows = at_rows(trace_rows(face_id, pair[which]))
                inner = [nodal[var, rows, :] for var in range(VARS)]
                outer = aligned[which]
                if axis_dir == 2:
                    outer = [
                        jnp.where(wall, -inner[var] if var == 1 + axis_dir else inner[var], outer[var])
                        for var in range(VARS)
                    ]
                flux_in, speed_in = side_terms(inner, axis_dir)
                flux_out, speed_out = side_terms(outer, axis_dir)
                wave = jnp.maximum(speed_in, speed_out)
                for var in range(VARS):
                    jump = sign_out * (flux_out[var] - flux_in[var]) - wave * (outer[var] - inner[var])
                    total[var, rows, :] = total[var, rows, :] + (0.5 * lift) * jump

    def layers_of(chunks):
        return [layer for chunk in chunks for layer in (2 * chunk, 2 * chunk + 1)]

    absorb(ORDER[0], True)
    absorb(ORDER[1], False)
    fetch_layers((0, 1), range(8))
    correct(0)
    correct(1)
    absorb(ORDER[2], False)
    fetch_layers((2, 3), layers_of(ORDER[:3]))
    for way in range(2):
        finish(way, rim_copy(way), rim_recv.at[way])
    scale = scale_at(0) + rim_recv[0, last, :] + rim_recv[1, last, :]
    traces = pl.ds(0, VARS * 8)
    blank = jnp.zeros((64 - VARS * 8, LANES), jnp.float32)
    rim_turned[...] = jnp.concatenate(
        [
            rim_own[0] + rim_recv[0, traces, :],
            blank,
            rim_own[1] + rim_recv[1, traces, :],
            blank,
        ],
        axis=0,
    ).T
    fetch_layers((4, 5), layers_of(ORDER[:3]))
    absorb(ORDER[3], False)
    fetch_layers((2, 3, 4, 5), layers_of(ORDER[3:]))
    for face_id in range(2, 6):
        correct(face_id)

    factor = jnp.broadcast_to((-TIME_STEP) * scale[:1, :], (LANES, LANES))
    for var in range(VARS):
        for chunk in range(CHUNKS):
            rows = pl.ds(chunk * LANES, LANES)
            result[var, :, rows] = (nodal[var, rows, :] + factor * total[var, rows, :]).T
    for way in range(2):

        @pl.when(sent[way])
        def _():
            for chunk in range(CHUNKS):
                chunk_copy(way, chunk).wait_send()
            rim_copy(way).wait_send()


def body(state_old, metric_old, new_position, partner, orient):
    matrix, weights = node_tables(POINTS)
    nodes = state_old.shape[2]
    rows_dev = partner.shape[1]
    cube = pltpu.VMEM((VARS, nodes, LANES), jnp.float32)
    advanced = pl.pallas_call(
        functools.partial(kernel, matrix, float(1.0 / weights[0])),
        out_shape=jax.ShapeDtypeStruct((VARS, rows_dev, nodes), jnp.float32),
        in_specs=[pl.BlockSpec(memory_space=pltpu.HBM)] * 6,
        out_specs=pl.BlockSpec(memory_space=pltpu.VMEM),
        scratch_shapes=[
            pltpu.SMEM((256,), jnp.int32),
            pltpu.VMEM((2, LANES), jnp.int32),
            pltpu.VMEM((2, LANES), jnp.float32),
            pltpu.VMEM((6, LANES), jnp.int32),
            pltpu.VMEM((6, LANES), jnp.int32),
        ]
        + [pltpu.VMEM((VARS, 2 * PAD, LANES), jnp.float32)] * CHUNKS
        + [
            pltpu.VMEM((2, CHUNKS, VARS, 64, LANES), jnp.float32),
            pltpu.VMEM((2, CHUNKS, VARS, 64, LANES), jnp.float32),
            pltpu.VMEM((2, VARS * 8 + 8, LANES), jnp.float32),
            pltpu.VMEM((2, VARS * 8 + 8, LANES), jnp.float32),
            pltpu.VMEM((2, VARS * 8, LANES), jnp.float32),
            pltpu.VMEM((LANES, LANES), jnp.float32),
        ]
        + [cube] * 6
        + [
            pltpu.VMEM((6, VARS, 64, LANES), jnp.float32),
            pltpu.SemaphoreType.DMA((CHUNKS,)),
            pltpu.SemaphoreType.DMA((5,)),
            pltpu.SemaphoreType.DMA((2, CHUNKS)),
            pltpu.SemaphoreType.DMA((2, CHUNKS)),
            pltpu.SemaphoreType.DMA((2,)),
            pltpu.SemaphoreType.DMA((2,)),
        ],
        compiler_params=pltpu.CompilerParams(
            collective_id=0, has_side_effects=True, vmem_limit_bytes=VMEM_LIMIT
        ),
    )(
        *[
            pltpu.with_memory_space_constraint(item, pltpu.HBM)
            for item in (
                new_position,
                new_position.reshape(2, LANES),
                metric_old.reshape(2, LANES),
                partner,
                orient,
                state_old.transpose(1, 0, 2),
            )
        ]
    )
    return advanced.transpose(1, 0, 2)


def solution(mesh):
    placed = (
        P(("curve", "sub"), None, None),
        P(("curve", "sub")),
        P(("curve", "sub")),
        P(None, ("curve", "sub")),
        P(None, ("curve", "sub")),
    )
    return jax.shard_map(
        body, mesh=mesh, in_specs=placed, out_specs=P(("curve", "sub"), None, None), check_vma=False
    )
```

```python
import functools

import jax
import jax.numpy as jnp
import numpy as np
from jax import lax
from jax.experimental import pallas as pl
from jax.experimental.pallas import tpu as pltpu
from jax.sharding import PartitionSpec as P

POINTS = 8
RIM = 16
VARS = 5
GAMMA = 1.4
TIME_STEP = 0.002
MESH = pl.DeviceIdType.MESH
CHUNKS = 4
ORDER = (0, 3, 1, 2)
PAD = 320
PIECE = 3
VMEM_LIMIT = 50 * 1024 * 1024
LANES = 128


def legendre_values(points, degree):
    previous = np.ones(points.shape)
    current = points.copy()
    for order_id in range(2, degree + 1):
        following = ((2 * order_id - 1) * points * current - (order_id - 1) * previous) / order_id
        previous = current
        current = following
    return (current, previous)


def lobatto_points(degree):
    points = np.cos(np.pi * np.arange(degree + 1) / degree)
    for sweep_id in range(100):
        current, previous = legendre_values(points, degree)
        points = points - (points * current - previous) / ((degree + 1) * current)
    points = points[::-1].copy()
    points[0] = -1.0
    points[degree] = 1.0
    return points


def node_tables(num_points):
    degree = num_points - 1
    points = lobatto_points(degree)
    values = legendre_values(points, degree)[0]
    weights = 2.0 / (degree * (degree + 1) * values**2)
    matrix = np.zeros((num_points, num_points))
    for row_pos in range(num_points):
        for col_pos in range(num_points):
            if row_pos != col_pos:
                matrix[row_pos, col_pos] = values[row_pos] / (
                    values[col_pos] * (points[row_pos] - points[col_pos])
                )
    matrix[0, 0] = -degree * (degree + 1) / 4.0
    matrix[degree, degree] = degree * (degree + 1) / 4.0
    return (matrix, weights)


def derivative(matrix, values):
    evens = [values[place] + values[7 - place] for place in range(4)]
    odds = [values[place] - values[7 - place] for place in range(4)]
    first, second = [], []
    for row in range(4):
        even, odd = [
            functools.reduce(
                lambda left, right: left + right,
                [
                    float(0.5 * (matrix[row, col] + sign * matrix[row, 7 - col])) * items[col]
                    for col in range(4)
                ],
            )
            for sign, items in ((1.0, evens), (-1.0, odds))
        ]
        first.append(even + odd)
        second.append(odd - even)
    return first + second[::-1]


def pick(values, index, axis):
    other = 1 - axis
    numbers = lax.GatherDimensionNumbers(
        offset_dims=(),
        collapsed_slice_dims=(axis,),
        start_index_map=(axis,),
        operand_batching_dims=(other,),
        start_indices_batching_dims=(other,),
    )
    return lax.gather(
        values, index[..., None], numbers, (1, 1), mode=lax.GatherScatterMode.PROMISE_IN_BOUNDS
    )


def trace_rows(face_id, layer):
    edge = 0 if face_id % 2 == 0 else POINTS - 1
    return ((edge * 64 + layer * 8, 1), (layer * 64 + edge * 8, 1), (layer * 64 + edge, 8))[face_id // 2]


def at_rows(rows):
    first, stride = rows
    return pl.ds(first, 8) if stride == 1 else pl.ds(first, 8, stride=stride)


def side_terms(state, axis_dir):
    density, energy = state[0], state[4]
    inverse = 1.0 / density
    momenta = state[1:4]
    kinetic = 0.5 * inverse * (momenta[0] * momenta[0] + momenta[1] * momenta[1] + momenta[2] * momenta[2])
    pressure = (GAMMA - 1.0) * (energy - kinetic)
    normal = momenta[axis_dir] * inverse
    speed = jnp.abs(normal) + jnp.sqrt(GAMMA * pressure * inverse)
    flux = [momenta[axis_dir]] + [item * normal for item in momenta] + [(energy + pressure) * normal]
    flux[1 + axis_dir] = flux[1 + axis_dir] + pressure
    return flux, speed


def kernel(
    matrix,
    lift,
    position_row_hbm,
    position_hbm,
    metric_hbm,
    partner_hbm,
    orient_hbm,
    state_hbm,
    result,
    first_ref,
    position_ref,
    metric_ref,
    partner_ref,
    orient_ref,
    staged_0,
    staged_1,
    staged_2,
    staged_3,
    send,
    recv,
    rim_send,
    rim_recv,
    rim_own,
    rim_turned,
    nodal,
    total,
    flux_x,
    flux_y,
    flux_z,
    slope_z,
    fetched,
    in_sem,
    table_sem,
    send_sem,
    recv_sem,
    rim_send_sem,
    rim_recv_sem,
    passing,
    pass_sem,
):
    sub_size = lax.axis_size("sub")
    devices = lax.axis_size("curve") * sub_size
    me = lax.axis_index("curve") * sub_size + lax.axis_index("sub")
    has_next, has_prev = me < devices - 1, me > 0
    after, before = jnp.minimum(me + 1, devices - 1), jnp.maximum(me - 1, 0)
    sides = ((after // sub_size, lax.rem(after, sub_size)), (before // sub_size, lax.rem(before, sub_size)))
    sent, arrives = (has_next, has_prev), (has_prev, has_next)

    plane = lax.axis_size("curve") * sub_size // 4
    spot_id, level = lax.rem(me, plane), me // plane
    is_low = (spot_id == plane - 1) & (level < 3)
    is_high = (spot_id == 0) & (level > 0)
    pass_up = (spot_id == sub_size - 1) & (level > 0)
    pass_down = (spot_id == plane - sub_size) & (level < 3)
    detours = (is_low, is_high)
    passes = (pass_up, pass_down)

    def mesh_place(device):
        device = jnp.clip(device, 0, devices - 1)
        return (device // sub_size, lax.rem(device, sub_size))

    passers = (mesh_place(me + sub_size), mesh_place(me - sub_size))
    sources = (mesh_place(me - sub_size), mesh_place(me + sub_size))
    drains = (mesh_place(me - sub_size + 1), mesh_place(me + sub_size - 1))
    fillers = (mesh_place(me + sub_size - 1), mesh_place(me - sub_size + 1))

    barrier = pltpu.get_barrier_semaphore()
    for way in range(2):

        @pl.when(sent[way])
        def _():
            pl.semaphore_signal(barrier, inc=1, device_id=sides[way], device_id_type=MESH)

        @pl.when(passes[way])
        def _():
            pl.semaphore_signal(barrier, inc=1, device_id=sources[way], device_id_type=MESH)

        @pl.when(detours[1 - way])
        def _():
            pl.semaphore_signal(barrier, inc=1, device_id=fillers[way], device_id_type=MESH)

    tables = [
        pltpu.make_async_copy(source, target, table_sem.at[place])
        for place, (source, target) in enumerate(
            (
                (position_row_hbm, first_ref),
                (position_hbm, position_ref),
                (metric_hbm, metric_ref),
                (partner_hbm, partner_ref),
                (orient_hbm, orient_ref),
            )
        )
    ]
    for copy in tables[:2]:
        copy.start()
    staged = (staged_0, staged_1, staged_2, staged_3)
    loads = [
        pltpu.make_async_copy(
            state_hbm.at[:, :, pl.ds(chunk * LANES, LANES)],
            staged[chunk].at[:, pl.ds(PAD, 256), :],
            in_sem.at[chunk],
        )
        for chunk in range(CHUNKS)
    ]
    for chunk in (ORDER[3],) + ORDER[:3]:
        loads[chunk].start()
    for copy in tables[2:]:
        copy.start()
    for copy in tables[:2]:
        copy.wait()

    shift = me * LANES - first_ref[0]
    start = PAD + jnp.clip(shift, -255, 128)
    alive = jnp.where(position_ref[...] >= 0, 1.0, 0.0)
    count = jnp.sum(alive).astype(jnp.int32)
    low, high = -shift, count - shift

    def rows_at(chunk, var, local, size):
        block = staged[chunk][var, pl.ds(start + local, size), :]
        row = local + lax.broadcasted_iota(jnp.int32, (size, LANES), 0)
        return jnp.where((row >= low) & (row < high), block, 0.0)

    def to_side(source, target, send_sems, recv_sems, way):
        return pltpu.make_async_remote_copy(
            src_ref=source,
            dst_ref=target,
            send_sem=send_sems,
            recv_sem=recv_sems,
            device_id=sides[way],
            device_id_type=MESH,
        )

    def start_if(way, copy):
        @pl.when(sent[way])
        def _():
            copy.start()

    def finish(way, copy, target):
        @pl.when(arrives[way])
        def _():
            copy.wait_recv()

        @pl.when(jnp.logical_not(arrives[way]))
        def _():
            target[...] = jnp.zeros(target.shape, jnp.float32)

    def chunk_copy(way, chunk):
        place = (way, chunk, pl.ds(PIECE, VARS - PIECE)) if chunk == ORDER[3] else (way, chunk)
        return to_side(send.at[place], recv.at[place], send_sem.at[way, chunk], recv_sem.at[way, chunk], way)

    def piece_copy(way, target=None, target_sem=None, device=None):
        place = (way, ORDER[3], pl.ds(0, PIECE))
        return pltpu.make_async_remote_copy(
            src_ref=send.at[place],
            dst_ref=recv.at[place] if target is None else target,
            send_sem=send_sem.at[way, CHUNKS],
            recv_sem=recv_sem.at[way, CHUNKS] if target is None else target_sem,
            device_id=sides[way] if target is None else device,
            device_id_type=MESH,
        )

    def send_detours():
        for way in range(2):

            @pl.when(detours[way])
            def _():
                piece_copy(way, passing, pass_sem.at[0], passers[way]).start()

    def send_direct():
        for way in range(2):

            @pl.when(sent[way] & jnp.logical_not(detours[way]))
            def _():
                piece_copy(way).start()

    def passed_copy(way):
        return pltpu.make_async_remote_copy(
            src_ref=passing,
            dst_ref=recv.at[way, ORDER[3], pl.ds(0, PIECE)],
            send_sem=pass_sem.at[1],
            recv_sem=recv_sem.at[way, CHUNKS],
            device_id=drains[way],
            device_id_type=MESH,
        )

    def pass_on():
        for way in range(2):

            @pl.when(passes[way])
            def _():
                piece_copy(way, passing, pass_sem.at[0], sides[way]).wait_recv()
                passed_copy(way).start()
                rim_copy(way).start()
                chunk_copy(way, ORDER[3]).start()

    def rim_copy(way):
        return to_side(rim_send.at[way], rim_recv.at[way], rim_send_sem.at[way], rim_recv_sem.at[way], way)

    def send_chunk(chunk):
        for way in range(2):
            start_if(way, chunk_copy(way, chunk))

    def build(chunk):
        loads[chunk].wait()
        for way, local in ((0, LANES), (1, -64)):
            for var in range(VARS):
                send[way, chunk, var] = rows_at(chunk, var, local, 64)

    build(ORDER[3])
    build(ORDER[0])
    peers = [has_next, has_prev, is_low, is_high, pass_up, pass_down]
    pl.semaphore_wait(barrier, sum([peer.astype(jnp.int32) for peer in peers], jnp.int32(0)))
    send_detours()
    send_chunk(ORDER[0])
    for chunk in ORDER[1:3]:
        build(chunk)
        send_chunk(chunk)
    for copy in tables[2:]:
        copy.wait()

    lane8 = lax.broadcasted_iota(jnp.int32, (8, LANES), 1)
    upper = lane8 >= 64
    piece = lax.rem(lane8, 64) // 16
    bottom = lax.rem(lane8, 16) * 8
    top = bottom + POINTS - 1
    for target, local, spot in (
        (rim_send.at[0], LANES - RIM, top),
        (rim_send.at[1], 0, bottom),
        (rim_own.at[0], -RIM, top),
        (rim_own.at[1], LANES, bottom),
    ):
        for var in range(VARS):
            value = None
            for chunk in range(CHUNKS):
                rows = rows_at(chunk, var, local, RIM)
                part = jnp.where(upper, pick(rows[8:], spot, 1), pick(rows[:8], spot, 1))
                value = part if value is None else jnp.where(piece == chunk, part, value)
            target[pl.ds(var * 8, 8), :] = value

    halves = [jnp.broadcast_to(metric_ref[pl.ds(half, 1), :], (8, LANES)) for half in range(2)]

    def scale_at(local):
        row = local + lane8
        index = row + shift
        value = jnp.where(index < LANES, pick(halves[0], index & 127, 1), pick(halves[1], index & 127, 1))
        return jnp.where((row >= low) & (row < high), value, 0.0)

    last = pl.ds(VARS * 8, 8)
    rim_send[0, last, :] = jnp.where(upper, 0.0, scale_at(LANES))
    rim_send[1, last, :] = jnp.where(upper, scale_at(-LANES), 0.0)

    send_direct()
    for way in range(2):

        @pl.when(sent[way] & jnp.logical_not(passes[way]))
        def _():
            rim_copy(way).start()
            chunk_copy(way, ORDER[3]).start()

    def absorb(chunk, first):
        for way in range(2):
            finish(way, chunk_copy(way, chunk), recv.at[way, chunk])
            if chunk == ORDER[3]:

                @pl.when(arrives[way])
                def _():
                    piece_copy(way).wait_recv()
        for var in range(VARS):
            moved = jnp.concatenate([recv[0, chunk, var], recv[1, chunk, var]], axis=0)
            nodal[var, pl.ds(chunk * LANES, LANES), :] = (rows_at(chunk, var, 0, LANES) + moved).T
        for part in range(8):
            rows = pl.ds(chunk * LANES + part * 16, 16)
            state = [nodal[var, rows, :] for var in range(VARS)]
            inverse = 1.0 / state[0]
            velocity = [item * inverse for item in state[1:4]]
            kinetic = 0.5 * (state[1] * velocity[0] + state[2] * velocity[1] + state[3] * velocity[2])
            pressure = (GAMMA - 1.0) * (state[4] - kinetic)
            enthalpy = state[4] + pressure
            for axis_dir, target in enumerate((flux_x, flux_y, flux_z)):
                flux = [state[1 + axis_dir]]
                for other in range(3):
                    product = state[1 + other] * velocity[axis_dir]
                    flux.append(product + pressure if other == axis_dir else product)
                flux.append(enthalpy * velocity[axis_dir])
                for var in range(VARS):
                    target[var, rows, :] = flux[var]
        layers = (2 * chunk, 2 * chunk + 1)
        for var in range(VARS):
            for layer in layers:
                base = layer * 64
                rows = [pl.ds(base + place, 8, stride=8) for place in range(8)]
                parts = derivative(matrix, [flux_z[var, rows[place], :] for place in range(8)])
                for place in range(8):
                    slope_z[var, rows[place], :] = parts[place]
            along_y = [
                derivative(matrix, [flux_y[var, pl.ds(layer * 64 + 8 * place, 8), :] for place in range(8)])
                for layer in layers
            ]
            for group in range(8):
                values = [flux_x[var, pl.ds(layer * 64 + 8 * group, 8), :] for layer in layers]
                for target in range(8):
                    rows = pl.ds(target * 64 + 8 * group, 8)
                    value = float(matrix[target, layers[0]]) * values[0]
                    value = value + float(matrix[target, layers[1]]) * values[1]
                    if target in layers:
                        value = value + along_y[target - layers[0]][group] + slope_z[var, rows, :]
                    total[var, rows, :] = value if first else total[var, rows, :] + value

    def across(face_id):
        partner = jnp.broadcast_to(partner_ref[pl.ds(face_id, 1), :], (8, LANES))
        return partner, partner & 127

    def fetch_layers(face_ids, layers):
        for face_id in face_ids:
            partner, local = across(face_id)
            away = (partner >> 7) != me
            for layer in layers:
                for var in range(VARS):
                    value = pick(nodal[var, at_rows(trace_rows(face_id ^ 1, layer)), :], local, 1)
                    if face_id >= 4:
                        index = (partner & 7) + var * 8 + (0 if face_id == 4 else 64)
                        other = jnp.where(
                            (partner & 8) == 0,
                            pick(rim_turned[pl.ds(layer * 8, 8), :], index, 1),
                            pick(rim_turned[pl.ds(64 + layer * 8, 8), :], index, 1),
                        )
                        value = jnp.where(away, other, value)
                    fetched[face_id, var, pl.ds(layer * 8, 8), :] = value

    row8 = lax.broadcasted_iota(jnp.int32, (8, LANES), 0)

    def correct(face_id):
        axis_dir, sign_out = face_id // 2, 1.0 if face_id % 2 else -1.0
        partner, _ = across(face_id)
        code = jnp.broadcast_to(orient_ref[pl.ds(face_id, 1), :], (8, LANES))
        turned = code >= 4
        flip_first = (code & 2) != 0
        flip_second = jnp.where((code & 1) != 0, 7 - row8, row8)
        wall = partner < 0
        for layer in range(4):
            pair = (layer, 7 - layer)
            aligned = [[], []]
            for var in range(VARS):
                near, far = [
                    jnp.where(
                        turned,
                        fetched[face_id, var, pl.ds(place, 8, stride=8), :],
                        fetched[face_id, var, pl.ds(place * 8, 8), :],
                    )
                    for place in pair
                ]
                aligned[0].append(pick(jnp.where(flip_first, far, near), flip_second, 0))
                aligned[1].append(pick(jnp.where(flip_first, near, far), flip_second, 0))
            for which in range(2):
                rows = at_rows(trace_rows(face_id, pair[which]))
                inner = [nodal[var, rows, :] for var in range(VARS)]
                outer = aligned[which]
                if axis_dir == 2:
                    outer = [
                        jnp.where(wall, -inner[var] if var == 1 + axis_dir else inner[var], outer[var])
                        for var in range(VARS)
                    ]
                flux_in, speed_in = side_terms(inner, axis_dir)
                flux_out, speed_out = side_terms(outer, axis_dir)
                wave = jnp.maximum(speed_in, speed_out)
                for var in range(VARS):
                    jump = sign_out * (flux_out[var] - flux_in[var]) - wave * (outer[var] - inner[var])
                    total[var, rows, :] = total[var, rows, :] + (0.5 * lift) * jump

    def layers_of(chunks):
        return [layer for chunk in chunks for layer in (2 * chunk, 2 * chunk + 1)]

    absorb(ORDER[0], True)
    pass_on()
    absorb(ORDER[1], False)
    fetch_layers((0, 1), range(8))
    correct(0)
    correct(1)
    absorb(ORDER[2], False)
    fetch_layers((2, 3), layers_of(ORDER[:3]))
    for way in range(2):
        finish(way, rim_copy(way), rim_recv.at[way])
    scale = scale_at(0) + rim_recv[0, last, :] + rim_recv[1, last, :]
    traces = pl.ds(0, VARS * 8)
    blank = jnp.zeros((64 - VARS * 8, LANES), jnp.float32)
    rim_turned[...] = jnp.concatenate(
        [
            rim_own[0] + rim_recv[0, traces, :],
            blank,
            rim_own[1] + rim_recv[1, traces, :],
            blank,
        ],
        axis=0,
    ).T
    fetch_layers((4, 5), layers_of(ORDER[:3]))
    absorb(ORDER[3], False)
    fetch_layers((2, 3, 4, 5), layers_of(ORDER[3:]))
    for face_id in range(2, 6):
        correct(face_id)

    factor = jnp.broadcast_to((-TIME_STEP) * scale[:1, :], (LANES, LANES))
    for var in range(VARS):
        for chunk in range(CHUNKS):
            rows = pl.ds(chunk * LANES, LANES)
            result[var, :, rows] = (nodal[var, rows, :] + factor * total[var, rows, :]).T
    for way in range(2):

        @pl.when(sent[way])
        def _():
            for chunk in range(CHUNKS):
                chunk_copy(way, chunk).wait_send()
            piece_copy(way).wait_send()
            rim_copy(way).wait_send()

        @pl.when(passes[way])
        def _():
            passed_copy(way).wait_send()


def body(state_old, metric_old, new_position, partner, orient):
    matrix, weights = node_tables(POINTS)
    nodes = state_old.shape[2]
    rows_dev = partner.shape[1]
    cube = pltpu.VMEM((VARS, nodes, LANES), jnp.float32)
    advanced = pl.pallas_call(
        functools.partial(kernel, matrix, float(1.0 / weights[0])),
        out_shape=jax.ShapeDtypeStruct((VARS, rows_dev, nodes), jnp.float32),
        in_specs=[pl.BlockSpec(memory_space=pltpu.HBM)] * 6,
        out_specs=pl.BlockSpec(memory_space=pltpu.VMEM),
        scratch_shapes=[
            pltpu.SMEM((256,), jnp.int32),
            pltpu.VMEM((2, LANES), jnp.int32),
            pltpu.VMEM((2, LANES), jnp.float32),
            pltpu.VMEM((6, LANES), jnp.int32),
            pltpu.VMEM((6, LANES), jnp.int32),
        ]
        + [pltpu.VMEM((VARS, 2 * PAD, LANES), jnp.float32)] * CHUNKS
        + [
            pltpu.VMEM((2, CHUNKS, VARS, 64, LANES), jnp.float32),
            pltpu.VMEM((2, CHUNKS, VARS, 64, LANES), jnp.float32),
            pltpu.VMEM((2, VARS * 8 + 8, LANES), jnp.float32),
            pltpu.VMEM((2, VARS * 8 + 8, LANES), jnp.float32),
            pltpu.VMEM((2, VARS * 8, LANES), jnp.float32),
            pltpu.VMEM((LANES, LANES), jnp.float32),
        ]
        + [cube] * 6
        + [
            pltpu.VMEM((6, VARS, 64, LANES), jnp.float32),
            pltpu.SemaphoreType.DMA((CHUNKS,)),
            pltpu.SemaphoreType.DMA((5,)),
            pltpu.SemaphoreType.DMA((2, CHUNKS + 1)),
            pltpu.SemaphoreType.DMA((2, CHUNKS + 1)),
            pltpu.SemaphoreType.DMA((2,)),
            pltpu.SemaphoreType.DMA((2,)),
            pltpu.VMEM((PIECE, 64, LANES), jnp.float32),
            pltpu.SemaphoreType.DMA((2,)),
        ],
        compiler_params=pltpu.CompilerParams(
            collective_id=0, has_side_effects=True, vmem_limit_bytes=VMEM_LIMIT
        ),
    )(
        *[
            pltpu.with_memory_space_constraint(item, pltpu.HBM)
            for item in (
                new_position,
                new_position.reshape(2, LANES),
                metric_old.reshape(2, LANES),
                partner,
                orient,
                state_old.transpose(1, 0, 2),
            )
        ]
    )
    return advanced.transpose(1, 0, 2)


def solution(mesh):
    placed = (
        P(("curve", "sub"), None, None),
        P(("curve", "sub")),
        P(("curve", "sub")),
        P(None, ("curve", "sub")),
        P(None, ("curve", "sub")),
    )
    return jax.shard_map(
        body, mesh=mesh, in_specs=placed, out_specs=P(("curve", "sub"), None, None), check_vma=False
    )
```

```python
import functools

import jax
import jax.numpy as jnp
import numpy as np
from jax import lax
from jax.experimental import pallas as pl
from jax.experimental.pallas import tpu as pltpu
from jax.sharding import PartitionSpec as P

POINTS = 8
RIM = 16
VARS = 5
GAMMA = 1.4
TIME_STEP = 0.002
MESH = pl.DeviceIdType.MESH
CHUNKS = 4
ORDER = (0, 3, 1, 2)
PAD = 320
PIECE = 3
VMEM_LIMIT = 50 * 1024 * 1024
LANES = 128


def legendre_values(points, degree):
    previous = np.ones(points.shape)
    current = points.copy()
    for order_id in range(2, degree + 1):
        following = ((2 * order_id - 1) * points * current - (order_id - 1) * previous) / order_id
        previous = current
        current = following
    return (current, previous)


def lobatto_points(degree):
    points = np.cos(np.pi * np.arange(degree + 1) / degree)
    for sweep_id in range(100):
        current, previous = legendre_values(points, degree)
        points = points - (points * current - previous) / ((degree + 1) * current)
    points = points[::-1].copy()
    points[0] = -1.0
    points[degree] = 1.0
    return points


def node_tables(num_points):
    degree = num_points - 1
    points = lobatto_points(degree)
    values = legendre_values(points, degree)[0]
    weights = 2.0 / (degree * (degree + 1) * values**2)
    matrix = np.zeros((num_points, num_points))
    for row_pos in range(num_points):
        for col_pos in range(num_points):
            if row_pos != col_pos:
                matrix[row_pos, col_pos] = values[row_pos] / (
                    values[col_pos] * (points[row_pos] - points[col_pos])
                )
    matrix[0, 0] = -degree * (degree + 1) / 4.0
    matrix[degree, degree] = degree * (degree + 1) / 4.0
    return (matrix, weights)


def derivative(matrix, values):
    evens = [values[place] + values[7 - place] for place in range(4)]
    odds = [values[place] - values[7 - place] for place in range(4)]
    first, second = [], []
    for row in range(4):
        even, odd = [
            functools.reduce(
                lambda left, right: left + right,
                [
                    float(0.5 * (matrix[row, col] + sign * matrix[row, 7 - col])) * items[col]
                    for col in range(4)
                ],
            )
            for sign, items in ((1.0, evens), (-1.0, odds))
        ]
        first.append(even + odd)
        second.append(odd - even)
    return first + second[::-1]


def pick(values, index, axis):
    other = 1 - axis
    numbers = lax.GatherDimensionNumbers(
        offset_dims=(),
        collapsed_slice_dims=(axis,),
        start_index_map=(axis,),
        operand_batching_dims=(other,),
        start_indices_batching_dims=(other,),
    )
    return lax.gather(
        values, index[..., None], numbers, (1, 1), mode=lax.GatherScatterMode.PROMISE_IN_BOUNDS
    )


def trace_rows(face_id, layer):
    edge = 0 if face_id % 2 == 0 else POINTS - 1
    return ((edge * 64 + layer * 8, 1), (layer * 64 + edge * 8, 1), (layer * 64 + edge, 8))[face_id // 2]


def at_rows(rows):
    first, stride = rows
    return pl.ds(first, 8) if stride == 1 else pl.ds(first, 8, stride=stride)


def side_terms(state, axis_dir):
    inverse = 1.0 / state[0]
    momenta = state[1:4]
    kinetic = 0.5 * inverse * (momenta[0] * momenta[0] + momenta[1] * momenta[1] + momenta[2] * momenta[2])
    pressure = (GAMMA - 1.0) * (state[4] - kinetic)
    normal = momenta[axis_dir] * inverse
    square = GAMMA * pressure * inverse
    speed = jnp.abs(normal) + square * lax.rsqrt(square)
    flux = [momenta[axis_dir]] + [item * normal for item in momenta] + [(state[4] + pressure) * normal]
    flux[1 + axis_dir] = flux[1 + axis_dir] + pressure
    return flux, speed


def kernel(
    matrix,
    lift,
    position_row_hbm,
    position_hbm,
    metric_hbm,
    partner_hbm,
    orient_hbm,
    state_hbm,
    result,
    first_ref,
    position_ref,
    metric_ref,
    partner_ref,
    orient_ref,
    staged_0,
    staged_1,
    staged_2,
    staged_3,
    send,
    recv,
    rim_send,
    rim_recv,
    rim_own,
    rim_turned,
    nodal,
    total,
    flux_x,
    flux_y,
    flux_z,
    slope_z,
    ends_z,
    speeds,
    fetched,
    in_sem,
    table_sem,
    send_sem,
    recv_sem,
    rim_send_sem,
    rim_recv_sem,
    passing,
    pass_sem,
):
    sub_size = lax.axis_size("sub")
    devices = lax.axis_size("curve") * sub_size
    me = lax.axis_index("curve") * sub_size + lax.axis_index("sub")
    has_next, has_prev = me < devices - 1, me > 0
    after, before = jnp.minimum(me + 1, devices - 1), jnp.maximum(me - 1, 0)
    sides = ((after // sub_size, lax.rem(after, sub_size)), (before // sub_size, lax.rem(before, sub_size)))
    sent, arrives = (has_next, has_prev), (has_prev, has_next)

    plane = lax.axis_size("curve") * sub_size // 4
    spot_id, level = lax.rem(me, plane), me // plane
    is_low = (spot_id == plane - 1) & (level < 3)
    is_high = (spot_id == 0) & (level > 0)
    pass_up = (spot_id == sub_size - 1) & (level > 0)
    pass_down = (spot_id == plane - sub_size) & (level < 3)
    detours = (is_low, is_high)
    passes = (pass_up, pass_down)

    def mesh_place(device):
        device = jnp.clip(device, 0, devices - 1)
        return (device // sub_size, lax.rem(device, sub_size))

    passers = (mesh_place(me + sub_size), mesh_place(me - sub_size))
    sources = (mesh_place(me - sub_size), mesh_place(me + sub_size))
    drains = (mesh_place(me - sub_size + 1), mesh_place(me + sub_size - 1))
    fillers = (mesh_place(me + sub_size - 1), mesh_place(me - sub_size + 1))

    barrier = pltpu.get_barrier_semaphore()
    for way in range(2):

        @pl.when(sent[way])
        def _():
            pl.semaphore_signal(barrier, inc=1, device_id=sides[way], device_id_type=MESH)

        @pl.when(passes[way])
        def _():
            pl.semaphore_signal(barrier, inc=1, device_id=sources[way], device_id_type=MESH)

        @pl.when(detours[1 - way])
        def _():
            pl.semaphore_signal(barrier, inc=1, device_id=fillers[way], device_id_type=MESH)

    tables = [
        pltpu.make_async_copy(source, target, table_sem.at[place])
        for place, (source, target) in enumerate(
            (
                (position_row_hbm, first_ref),
                (position_hbm, position_ref),
                (metric_hbm, metric_ref),
                (partner_hbm, partner_ref),
                (orient_hbm, orient_ref),
            )
        )
    ]
    for copy in tables[:2]:
        copy.start()
    staged = (staged_0, staged_1, staged_2, staged_3)
    loads = [
        pltpu.make_async_copy(
            state_hbm.at[:, :, pl.ds(chunk * LANES, LANES)],
            staged[chunk].at[:, pl.ds(PAD, 256), :],
            in_sem.at[chunk],
        )
        for chunk in range(CHUNKS)
    ]
    for chunk in (ORDER[3],) + ORDER[:3]:
        loads[chunk].start()
    for copy in tables[2:]:
        copy.start()
    for copy in tables[:2]:
        copy.wait()

    shift = me * LANES - first_ref[0]
    start = PAD + jnp.clip(shift, -255, 128)
    alive = jnp.where(position_ref[...] >= 0, 1.0, 0.0)
    count = jnp.sum(alive).astype(jnp.int32)
    low, high = -shift, count - shift

    def rows_at(chunk, var, local, size):
        block = staged[chunk][var, pl.ds(start + local, size), :]
        row = local + lax.broadcasted_iota(jnp.int32, (size, LANES), 0)
        return jnp.where((row >= low) & (row < high), block, 0.0)

    def to_side(source, target, send_sems, recv_sems, way):
        return pltpu.make_async_remote_copy(
            src_ref=source,
            dst_ref=target,
            send_sem=send_sems,
            recv_sem=recv_sems,
            device_id=sides[way],
            device_id_type=MESH,
        )

    def start_if(way, copy):
        @pl.when(sent[way])
        def _():
            copy.start()

    def finish(way, copy, target):
        @pl.when(arrives[way])
        def _():
            copy.wait_recv()

        @pl.when(jnp.logical_not(arrives[way]))
        def _():
            target[...] = jnp.zeros(target.shape, jnp.float32)

    def chunk_copy(way, chunk):
        place = (way, chunk, pl.ds(PIECE, VARS - PIECE)) if chunk == ORDER[3] else (way, chunk)
        return to_side(send.at[place], recv.at[place], send_sem.at[way, chunk], recv_sem.at[way, chunk], way)

    def piece_copy(way, target=None, target_sem=None, device=None):
        place = (way, ORDER[3], pl.ds(0, PIECE))
        return pltpu.make_async_remote_copy(
            src_ref=send.at[place],
            dst_ref=recv.at[place] if target is None else target,
            send_sem=send_sem.at[way, CHUNKS],
            recv_sem=recv_sem.at[way, CHUNKS] if target is None else target_sem,
            device_id=sides[way] if target is None else device,
            device_id_type=MESH,
        )

    def send_detours():
        for way in range(2):

            @pl.when(detours[way])
            def _():
                piece_copy(way, passing, pass_sem.at[0], passers[way]).start()

    def send_direct():
        for way in range(2):

            @pl.when(sent[way] & jnp.logical_not(detours[way]))
            def _():
                piece_copy(way).start()

    def passed_copy(way):
        return pltpu.make_async_remote_copy(
            src_ref=passing,
            dst_ref=recv.at[way, ORDER[3], pl.ds(0, PIECE)],
            send_sem=pass_sem.at[1],
            recv_sem=recv_sem.at[way, CHUNKS],
            device_id=drains[way],
            device_id_type=MESH,
        )

    def pass_on():
        for way in range(2):

            @pl.when(passes[way])
            def _():
                piece_copy(way, passing, pass_sem.at[0], sides[way]).wait_recv()
                passed_copy(way).start()
                chunk_copy(way, ORDER[3]).start()

    def rim_copy(way):
        return to_side(rim_send.at[way], rim_recv.at[way], rim_send_sem.at[way], rim_recv_sem.at[way], way)

    def send_chunk(chunk):
        for way in range(2):
            start_if(way, chunk_copy(way, chunk))

    def build(chunk):
        loads[chunk].wait()
        for way, local in ((0, LANES), (1, -64)):
            for var in range(VARS):
                send[way, chunk, var] = rows_at(chunk, var, local, 64)

    build(ORDER[3])
    build(ORDER[0])
    peers = [has_next, has_prev, is_low, is_high, pass_up, pass_down]
    pl.semaphore_wait(barrier, sum([peer.astype(jnp.int32) for peer in peers], jnp.int32(0)))
    send_detours()
    send_chunk(ORDER[0])
    build(ORDER[1])
    send_chunk(ORDER[1])
    build(ORDER[2])
    for copy in tables[2:]:
        copy.wait()

    lane8 = lax.broadcasted_iota(jnp.int32, (8, LANES), 1)
    upper = lane8 >= 64
    piece = lax.rem(lane8, 64) // 16
    bottom = lax.rem(lane8, 16) * 8
    top = bottom + POINTS - 1
    for target, local, spot in (
        (rim_send.at[0], LANES - RIM, top),
        (rim_send.at[1], 0, bottom),
        (rim_own.at[0], -RIM, top),
        (rim_own.at[1], LANES, bottom),
    ):
        for var in range(VARS):
            value = None
            for chunk in range(CHUNKS):
                rows = rows_at(chunk, var, local, RIM)
                part = jnp.where(upper, pick(rows[8:], spot, 1), pick(rows[:8], spot, 1))
                value = part if value is None else jnp.where(piece == chunk, part, value)
            target[pl.ds(var * 8, 8), :] = value

    halves = [jnp.broadcast_to(metric_ref[pl.ds(half, 1), :], (8, LANES)) for half in range(2)]

    def scale_at(local):
        row = local + lane8
        index = row + shift
        value = jnp.where(index < LANES, pick(halves[0], index & 127, 1), pick(halves[1], index & 127, 1))
        return jnp.where((row >= low) & (row < high), value, 0.0)

    last = pl.ds(VARS * 8, 8)
    rim_send[0, last, :] = jnp.where(upper, 0.0, scale_at(LANES))
    rim_send[1, last, :] = jnp.where(upper, scale_at(-LANES), 0.0)

    for way in range(2):
        start_if(way, rim_copy(way))
    send_chunk(ORDER[2])
    send_direct()
    for way in range(2):

        @pl.when(sent[way] & jnp.logical_not(passes[way]))
        def _():
            chunk_copy(way, ORDER[3]).start()

    def absorb(chunk, first=False, last_one=False):
        def place(variables):
            for var in variables:
                moved = jnp.concatenate([recv[0, chunk, var], recv[1, chunk, var]], axis=0)
                nodal[var, pl.ds(chunk * LANES, LANES), :] = (rows_at(chunk, var, 0, LANES) + moved).T

        if chunk == ORDER[3]:
            for way in range(2):
                finish(way, piece_copy(way), recv.at[way, chunk, pl.ds(0, PIECE)])
            place(range(PIECE))
            for way in range(2):
                finish(way, chunk_copy(way, chunk), recv.at[way, chunk, pl.ds(PIECE, VARS - PIECE)])
            place(range(PIECE, VARS))
        else:
            for way in range(2):
                finish(way, chunk_copy(way, chunk), recv.at[way, chunk])
            place(range(VARS))
        for part in range(8):
            rows = pl.ds(chunk * LANES + part * 16, 16)
            state = [nodal[var, rows, :] for var in range(VARS)]
            momenta = state[1:4]
            inverse = 1.0 / state[0]
            velocity = [item * inverse for item in momenta]
            product = [[None] * 3 for _ in range(3)]
            for row in range(3):
                for col in range(row, 3):
                    product[row][col] = product[col][row] = momenta[row] * velocity[col]
            kinetic = 0.5 * (product[0][0] + product[1][1] + product[2][2])
            pressure = (GAMMA - 1.0) * (state[4] - kinetic)
            enthalpy = state[4] + pressure
            square = GAMMA * pressure * inverse
            sound = square * lax.rsqrt(square)
            for axis_dir, target in enumerate((flux_x, flux_y, flux_z)):
                target[0, rows, :] = momenta[axis_dir]
                for other in range(3):
                    value = product[axis_dir][other]
                    target[1 + other, rows, :] = value + pressure if other == axis_dir else value
                target[4, rows, :] = enthalpy * velocity[axis_dir]
                if axis_dir < 2:
                    speeds[axis_dir, rows, :] = jnp.abs(velocity[axis_dir]) + sound
        layers = (2 * chunk, 2 * chunk + 1)
        for side in range(2):
            for layer in layers:
                for var in range(VARS):
                    ends_z[side, var, pl.ds(layer * 8, 8), :] = nodal[
                        var, at_rows(trace_rows(4 + side, layer)), :
                    ]
        for var in range(VARS):
            for layer in layers:
                base = layer * 64
                rows = [pl.ds(base + place, 8, stride=8) for place in range(8)]
                parts = derivative(matrix, [flux_z[var, rows[place], :] for place in range(8)])
                for place in range(8):
                    slope_z[var, rows[place], :] = parts[place]
            along_y = [
                derivative(matrix, [flux_y[var, pl.ds(layer * 64 + 8 * place, 8), :] for place in range(8)])
                for layer in layers
            ]
            for group in range(8):
                values = [flux_x[var, pl.ds(layer * 64 + 8 * group, 8), :] for layer in layers]
                for target in layers if last_one else range(8):
                    rows = pl.ds(target * 64 + 8 * group, 8)
                    terms = [] if first else [total[var, rows, :]]
                    if not last_one:
                        terms += [float(matrix[target, layer]) * value for layer, value in zip(layers, values)]
                    if target in layers:
                        terms += [along_y[target - layers[0]][group], slope_z[var, rows, :]]
                    total[var, rows, :] = functools.reduce(lambda left, right: left + right, terms)

    def across(face_id):
        partner = jnp.broadcast_to(partner_ref[pl.ds(face_id, 1), :], (8, LANES))
        return partner, partner & 127

    def fetch_layers(face_ids, layers):
        for face_id in face_ids:
            partner, local = across(face_id)
            away = (partner >> 7) != me
            for layer in layers:
                for var in range(VARS):
                    if face_id < 4:
                        value = nodal[var, at_rows(trace_rows(face_id ^ 1, layer)), :]
                    else:
                        value = ends_z[5 - face_id, var, pl.ds(layer * 8, 8), :]
                    value = pick(value, local, 1)
                    if face_id >= 4:
                        index = (partner & 7) + var * 8 + (0 if face_id == 4 else 64)
                        other = jnp.where(
                            (partner & 8) == 0,
                            pick(rim_turned[pl.ds(layer * 8, 8), :], index, 1),
                            pick(rim_turned[pl.ds(64 + layer * 8, 8), :], index, 1),
                        )
                        value = jnp.where(away, other, value)
                    fetched[face_id, var, pl.ds(layer * 8, 8), :] = value

    row8 = lax.broadcasted_iota(jnp.int32, (8, LANES), 0)

    def correct(face_id):
        axis_dir, sign_out = face_id // 2, 1.0 if face_id % 2 else -1.0
        partner, _ = across(face_id)
        code = jnp.broadcast_to(orient_ref[pl.ds(face_id, 1), :], (8, LANES))
        turned = code >= 4
        flip_first = (code & 2) != 0
        flip_second = jnp.where((code & 1) != 0, 7 - row8, row8)
        wall = partner < 0
        inner_flux = (flux_x, flux_y, None)[axis_dir]
        for layer in range(4):
            pair = (layer, 7 - layer)
            aligned = [[], []]
            for var in range(VARS):
                near, far = [
                    jnp.where(
                        turned,
                        fetched[face_id, var, pl.ds(place, 8, stride=8), :],
                        fetched[face_id, var, pl.ds(place * 8, 8), :],
                    )
                    for place in pair
                ]
                aligned[0].append(pick(jnp.where(flip_first, far, near), flip_second, 0))
                aligned[1].append(pick(jnp.where(flip_first, near, far), flip_second, 0))
            for which in range(2):
                rows = at_rows(trace_rows(face_id, pair[which]))
                outer = aligned[which]
                if axis_dir == 2:
                    layer_rows = pl.ds(pair[which] * 8, 8)
                    inner = [ends_z[face_id - 4, var, layer_rows, :] for var in range(VARS)]
                    outer = [
                        jnp.where(wall, -inner[var] if var == 1 + axis_dir else inner[var], outer[var])
                        for var in range(VARS)
                    ]
                    flux_in, speed_in = side_terms(inner, axis_dir)
                else:
                    inner = [nodal[var, rows, :] for var in range(VARS)]
                    flux_in = [inner_flux[var, rows, :] for var in range(VARS)]
                    speed_in = speeds[axis_dir, rows, :]
                flux_out, speed_out = side_terms(outer, axis_dir)
                wave = jnp.maximum(speed_in, speed_out)
                for var in range(VARS):
                    jump = flux_out[var] - flux_in[var] if sign_out > 0 else flux_in[var] - flux_out[var]
                    total[var, rows, :] = total[var, rows, :] + (jump - wave * (outer[var] - inner[var]))

    def layers_of(chunks):
        return [layer for chunk in chunks for layer in (2 * chunk, 2 * chunk + 1)]

    absorb(ORDER[0], first=True)
    pass_on()
    absorb(ORDER[1])
    fetch_layers((0, 1), range(8))
    correct(0)
    correct(1)
    fetch_layers((2, 3), layers_of(ORDER[:2]))
    for way in range(2):
        finish(way, rim_copy(way), rim_recv.at[way])
    scale = scale_at(0) + rim_recv[0, last, :] + rim_recv[1, last, :]
    traces = pl.ds(0, VARS * 8)
    blank = jnp.zeros((64 - VARS * 8, LANES), jnp.float32)
    rim_turned[...] = jnp.concatenate(
        [
            rim_own[0] + rim_recv[0, traces, :],
            blank,
            rim_own[1] + rim_recv[1, traces, :],
            blank,
        ],
        axis=0,
    ).T
    fetch_layers((4, 5), layers_of(ORDER[:2]))
    absorb(ORDER[2])
    fetch_layers((2, 3, 4, 5), layers_of(ORDER[2:3]))
    absorb(ORDER[3], last_one=True)
    fetch_layers((2, 3, 4, 5), layers_of(ORDER[3:]))
    for face_id in range(2, 6):
        correct(face_id)

    factor = jnp.broadcast_to((-TIME_STEP * lift) * scale[:1, :], (64, LANES))
    late = layers_of(ORDER[3:])
    for var in range(VARS):
        values = [flux_x[var, pl.ds(layer * 64, 64), :] for layer in late]
        for chunk in range(CHUNKS):
            blocks = []
            for target in layers_of((chunk,)):
                rows = pl.ds(target * 64, 64)
                slope = total[var, rows, :]
                for layer, value in zip(late, values):
                    slope = slope + float(matrix[target, layer]) * value
                blocks.append(nodal[var, rows, :] + factor * slope)
            result[var, :, pl.ds(chunk * LANES, LANES)] = jnp.concatenate(blocks, axis=0).T
    for way in range(2):

        @pl.when(sent[way])
        def _():
            for chunk in range(CHUNKS):
                chunk_copy(way, chunk).wait_send()
            piece_copy(way).wait_send()
            rim_copy(way).wait_send()

        @pl.when(passes[way])
        def _():
            passed_copy(way).wait_send()


def body(state_old, metric_old, new_position, partner, orient):
    matrix, weights = node_tables(POINTS)
    nodes = state_old.shape[2]
    rows_dev = partner.shape[1]
    cube = pltpu.VMEM((VARS, nodes, LANES), jnp.float32)
    advanced = pl.pallas_call(
        functools.partial(kernel, matrix * (2.0 * weights[0]), float(0.5 / weights[0])),
        out_shape=jax.ShapeDtypeStruct((VARS, rows_dev, nodes), jnp.float32),
        in_specs=[pl.BlockSpec(memory_space=pltpu.HBM)] * 6,
        out_specs=pl.BlockSpec(memory_space=pltpu.VMEM),
        scratch_shapes=[
            pltpu.SMEM((256,), jnp.int32),
            pltpu.VMEM((2, LANES), jnp.int32),
            pltpu.VMEM((2, LANES), jnp.float32),
            pltpu.VMEM((6, LANES), jnp.int32),
            pltpu.VMEM((6, LANES), jnp.int32),
        ]
        + [pltpu.VMEM((VARS, 2 * PAD, LANES), jnp.float32)] * CHUNKS
        + [
            pltpu.VMEM((2, CHUNKS, VARS, 64, LANES), jnp.float32),
            pltpu.VMEM((2, CHUNKS, VARS, 64, LANES), jnp.float32),
            pltpu.VMEM((2, VARS * 8 + 8, LANES), jnp.float32),
            pltpu.VMEM((2, VARS * 8 + 8, LANES), jnp.float32),
            pltpu.VMEM((2, VARS * 8, LANES), jnp.float32),
            pltpu.VMEM((LANES, LANES), jnp.float32),
        ]
        + [cube] * 6
        + [
            pltpu.VMEM((2, VARS, 64, LANES), jnp.float32),
            pltpu.VMEM((2, nodes, LANES), jnp.float32),
            pltpu.VMEM((6, VARS, 64, LANES), jnp.float32),
            pltpu.SemaphoreType.DMA((CHUNKS,)),
            pltpu.SemaphoreType.DMA((5,)),
            pltpu.SemaphoreType.DMA((2, CHUNKS + 1)),
            pltpu.SemaphoreType.DMA((2, CHUNKS + 1)),
            pltpu.SemaphoreType.DMA((2,)),
            pltpu.SemaphoreType.DMA((2,)),
            pltpu.VMEM((PIECE, 64, LANES), jnp.float32),
            pltpu.SemaphoreType.DMA((2,)),
        ],
        compiler_params=pltpu.CompilerParams(
            collective_id=0, has_side_effects=True, vmem_limit_bytes=VMEM_LIMIT
        ),
    )(
        *[
            pltpu.with_memory_space_constraint(item, pltpu.HBM)
            for item in (
                new_position,
                new_position.reshape(2, LANES),
                metric_old.reshape(2, LANES),
                partner,
                orient,
                state_old.transpose(1, 0, 2),
            )
        ]
    )
    return advanced.transpose(1, 0, 2)


def solution(mesh):
    placed = (
        P(("curve", "sub"), None, None),
        P(("curve", "sub")),
        P(("curve", "sub")),
        P(None, ("curve", "sub")),
        P(None, ("curve", "sub")),
    )
    return jax.shard_map(
        body, mesh=mesh, in_specs=placed, out_specs=P(("curve", "sub"), None, None), check_vma=False
    )
```

```python
import functools

import jax
import jax.numpy as jnp
import numpy as np
from jax import lax
from jax.experimental import pallas as pl
from jax.experimental.pallas import tpu as pltpu
from jax.sharding import PartitionSpec as P

POINTS = 8
RIM = 16
VARS = 5
GAMMA = 1.4
TIME_STEP = 0.002
MESH = pl.DeviceIdType.MESH
CHUNKS = 4
ORDER = (0, 3, 1, 2)
PAD = 320
PIECE = 3
VMEM_LIMIT = 50 * 1024 * 1024
LANES = 128


def legendre_values(points, degree):
    previous = np.ones(points.shape)
    current = points.copy()
    for order_id in range(2, degree + 1):
        following = ((2 * order_id - 1) * points * current - (order_id - 1) * previous) / order_id
        previous = current
        current = following
    return (current, previous)


def lobatto_points(degree):
    points = np.cos(np.pi * np.arange(degree + 1) / degree)
    for sweep_id in range(100):
        current, previous = legendre_values(points, degree)
        points = points - (points * current - previous) / ((degree + 1) * current)
    points = points[::-1].copy()
    points[0] = -1.0
    points[degree] = 1.0
    return points


def node_tables(num_points):
    degree = num_points - 1
    points = lobatto_points(degree)
    values = legendre_values(points, degree)[0]
    weights = 2.0 / (degree * (degree + 1) * values**2)
    matrix = np.zeros((num_points, num_points))
    for row_pos in range(num_points):
        for col_pos in range(num_points):
            if row_pos != col_pos:
                matrix[row_pos, col_pos] = values[row_pos] / (
                    values[col_pos] * (points[row_pos] - points[col_pos])
                )
    matrix[0, 0] = -degree * (degree + 1) / 4.0
    matrix[degree, degree] = degree * (degree + 1) / 4.0
    return (matrix, weights)


def derivative(matrix, values):
    evens = [values[place] + values[7 - place] for place in range(4)]
    odds = [values[place] - values[7 - place] for place in range(4)]
    first, second = [], []
    for row in range(4):
        even, odd = [
            functools.reduce(
                lambda left, right: left + right,
                [
                    float(0.5 * (matrix[row, col] + sign * matrix[row, 7 - col])) * items[col]
                    for col in range(4)
                ],
            )
            for sign, items in ((1.0, evens), (-1.0, odds))
        ]
        first.append(even + odd)
        second.append(odd - even)
    return first + second[::-1]


def pick(values, index, axis):
    other = 1 - axis
    numbers = lax.GatherDimensionNumbers(
        offset_dims=(),
        collapsed_slice_dims=(axis,),
        start_index_map=(axis,),
        operand_batching_dims=(other,),
        start_indices_batching_dims=(other,),
    )
    return lax.gather(
        values, index[..., None], numbers, (1, 1), mode=lax.GatherScatterMode.PROMISE_IN_BOUNDS
    )


def trace_rows(face_id, layer):
    edge = 0 if face_id % 2 == 0 else POINTS - 1
    return ((edge * 64 + layer * 8, 1), (layer * 64 + edge * 8, 1), (layer * 64 + edge, 8))[face_id // 2]


def at_rows(rows):
    first, stride = rows
    return pl.ds(first, 8) if stride == 1 else pl.ds(first, 8, stride=stride)


def side_terms(state, axis_dir):
    inverse = 1.0 / state[0]
    momenta = state[1:4]
    kinetic = 0.5 * inverse * (momenta[0] * momenta[0] + momenta[1] * momenta[1] + momenta[2] * momenta[2])
    pressure = (GAMMA - 1.0) * (state[4] - kinetic)
    normal = momenta[axis_dir] * inverse
    square = GAMMA * pressure * inverse
    speed = jnp.abs(normal) + square * lax.rsqrt(square)
    flux = [momenta[axis_dir]] + [item * normal for item in momenta] + [(state[4] + pressure) * normal]
    flux[1 + axis_dir] = flux[1 + axis_dir] + pressure
    return flux, speed


def kernel(
    matrix,
    lift,
    position_row_hbm,
    position_hbm,
    metric_hbm,
    partner_hbm,
    orient_hbm,
    state_hbm,
    result,
    first_ref,
    position_ref,
    metric_ref,
    partner_ref,
    orient_ref,
    staged_0,
    staged_1,
    staged_2,
    staged_3,
    send,
    recv,
    rim_send,
    rim_recv,
    rim_own,
    rim_turned,
    nodal,
    total,
    flux_x,
    flux_y,
    flux_z,
    slope_z,
    ends_z,
    speeds,
    fetched,
    in_sem,
    table_sem,
    send_sem,
    recv_sem,
    rim_send_sem,
    rim_recv_sem,
    passing,
    pass_sem,
):
    sub_size = lax.axis_size("sub")
    devices = lax.axis_size("curve") * sub_size
    me = lax.axis_index("curve") * sub_size + lax.axis_index("sub")
    has_next, has_prev = me < devices - 1, me > 0
    after, before = jnp.minimum(me + 1, devices - 1), jnp.maximum(me - 1, 0)
    sides = ((after // sub_size, lax.rem(after, sub_size)), (before // sub_size, lax.rem(before, sub_size)))
    sent, arrives = (has_next, has_prev), (has_prev, has_next)

    plane = lax.axis_size("curve") * sub_size // 4
    spot_id, level = lax.rem(me, plane), me // plane
    is_low = (spot_id == plane - 1) & (level < 3)
    is_high = (spot_id == 0) & (level > 0)
    pass_up = (spot_id == sub_size - 1) & (level > 0)
    pass_down = (spot_id == plane - sub_size) & (level < 3)
    detours = (is_low, is_high)
    passes = (pass_up, pass_down)

    def mesh_place(device):
        device = jnp.clip(device, 0, devices - 1)
        return (device // sub_size, lax.rem(device, sub_size))

    passers = (mesh_place(me + sub_size), mesh_place(me - sub_size))
    sources = (mesh_place(me - sub_size), mesh_place(me + sub_size))
    drains = (mesh_place(me - sub_size + 1), mesh_place(me + sub_size - 1))
    fillers = (mesh_place(me + sub_size - 1), mesh_place(me - sub_size + 1))

    barrier = pltpu.get_barrier_semaphore()
    for way in range(2):

        @pl.when(sent[way])
        def _():
            pl.semaphore_signal(barrier, inc=1, device_id=sides[way], device_id_type=MESH)

        @pl.when(passes[way])
        def _():
            pl.semaphore_signal(barrier, inc=1, device_id=sources[way], device_id_type=MESH)

        @pl.when(detours[1 - way])
        def _():
            pl.semaphore_signal(barrier, inc=1, device_id=fillers[way], device_id_type=MESH)

    tables = [
        pltpu.make_async_copy(source, target, table_sem.at[place])
        for place, (source, target) in enumerate(
            (
                (position_row_hbm, first_ref),
                (position_hbm, position_ref),
                (metric_hbm, metric_ref),
                (partner_hbm, partner_ref),
                (orient_hbm, orient_ref),
            )
        )
    ]
    for copy in tables[:2]:
        copy.start()
    staged = (staged_0, staged_1, staged_2, staged_3)
    loads = [
        pltpu.make_async_copy(
            state_hbm.at[:, :, pl.ds(chunk * LANES, LANES)],
            staged[chunk].at[:, pl.ds(PAD, 256), :],
            in_sem.at[chunk],
        )
        for chunk in range(CHUNKS)
    ]
    for chunk in (ORDER[3],) + ORDER[:3]:
        loads[chunk].start()
    for copy in tables[2:]:
        copy.start()
    for copy in tables[:2]:
        copy.wait()

    shift = me * LANES - first_ref[0]
    start = PAD + jnp.clip(shift, -255, 128)
    alive = jnp.where(position_ref[...] >= 0, 1.0, 0.0)
    count = jnp.sum(alive).astype(jnp.int32)
    low, high = -shift, count - shift

    def rows_at(chunk, var, local, size):
        block = staged[chunk][var, pl.ds(start + local, size), :]
        row = local + lax.broadcasted_iota(jnp.int32, (size, LANES), 0)
        return jnp.where((row >= low) & (row < high), block, 0.0)

    def to_side(source, target, send_sems, recv_sems, way):
        return pltpu.make_async_remote_copy(
            src_ref=source,
            dst_ref=target,
            send_sem=send_sems,
            recv_sem=recv_sems,
            device_id=sides[way],
            device_id_type=MESH,
        )

    def start_if(way, copy):
        @pl.when(sent[way])
        def _():
            copy.start()

    def finish(way, copy, target):
        @pl.when(arrives[way])
        def _():
            copy.wait_recv()

        @pl.when(jnp.logical_not(arrives[way]))
        def _():
            target[...] = jnp.zeros(target.shape, jnp.float32)

    def chunk_copy(way, chunk):
        place = (way, chunk, pl.ds(PIECE, VARS - PIECE)) if chunk == ORDER[3] else (way, chunk)
        return to_side(send.at[place], recv.at[place], send_sem.at[way, chunk], recv_sem.at[way, chunk], way)

    def piece_copy(way, target=None, target_sem=None, device=None):
        place = (way, ORDER[3], pl.ds(0, PIECE))
        return pltpu.make_async_remote_copy(
            src_ref=send.at[place],
            dst_ref=recv.at[place] if target is None else target,
            send_sem=send_sem.at[way, CHUNKS],
            recv_sem=recv_sem.at[way, CHUNKS] if target is None else target_sem,
            device_id=sides[way] if target is None else device,
            device_id_type=MESH,
        )

    def send_detours():
        for way in range(2):

            @pl.when(detours[way])
            def _():
                piece_copy(way, passing, pass_sem.at[0], passers[way]).start()

    def send_direct():
        for way in range(2):

            @pl.when(sent[way] & jnp.logical_not(detours[way]))
            def _():
                piece_copy(way).start()

    def passed_copy(way):
        return pltpu.make_async_remote_copy(
            src_ref=passing,
            dst_ref=recv.at[way, ORDER[3], pl.ds(0, PIECE)],
            send_sem=pass_sem.at[1],
            recv_sem=recv_sem.at[way, CHUNKS],
            device_id=drains[way],
            device_id_type=MESH,
        )

    def pass_on():
        for way in range(2):

            @pl.when(passes[way])
            def _():
                piece_copy(way, passing, pass_sem.at[0], sides[way]).wait_recv()
                passed_copy(way).start()
                chunk_copy(way, ORDER[3]).start()

    def rim_copy(way):
        return to_side(rim_send.at[way], rim_recv.at[way], rim_send_sem.at[way], rim_recv_sem.at[way], way)

    def send_chunk(chunk):
        for way in range(2):
            start_if(way, chunk_copy(way, chunk))

    def build(chunk):
        loads[chunk].wait()
        for way, local in ((0, LANES), (1, -64)):
            for var in range(VARS):
                send[way, chunk, var] = rows_at(chunk, var, local, 64)

    build(ORDER[3])
    build(ORDER[0])
    peers = [has_next, has_prev, is_low, is_high, pass_up, pass_down]
    pl.semaphore_wait(barrier, sum([peer.astype(jnp.int32) for peer in peers], jnp.int32(0)))
    send_detours()
    send_chunk(ORDER[0])
    build(ORDER[1])
    send_chunk(ORDER[1])
    build(ORDER[2])
    for copy in tables[2:]:
        copy.wait()

    lane8 = lax.broadcasted_iota(jnp.int32, (8, LANES), 1)
    upper = lane8 >= 64
    piece = lax.rem(lane8, 64) // 16
    bottom = lax.rem(lane8, 16) * 8
    top = bottom + POINTS - 1
    for target, local, spot in (
        (rim_send.at[0], LANES - RIM, top),
        (rim_send.at[1], 0, bottom),
        (rim_own.at[0], -RIM, top),
        (rim_own.at[1], LANES, bottom),
    ):
        for var in range(VARS):
            value = None
            for chunk in range(CHUNKS):
                rows = rows_at(chunk, var, local, RIM)
                part = jnp.where(upper, pick(rows[8:], spot, 1), pick(rows[:8], spot, 1))
                value = part if value is None else jnp.where(piece == chunk, part, value)
            target[pl.ds(var * 8, 8), :] = value

    halves = [jnp.broadcast_to(metric_ref[pl.ds(half, 1), :], (8, LANES)) for half in range(2)]

    def scale_at(local):
        row = local + lane8
        index = row + shift
        value = jnp.where(index < LANES, pick(halves[0], index & 127, 1), pick(halves[1], index & 127, 1))
        return jnp.where((row >= low) & (row < high), value, 0.0)

    last = pl.ds(VARS * 8, 8)
    rim_send[0, last, :] = jnp.where(upper, 0.0, scale_at(LANES))
    rim_send[1, last, :] = jnp.where(upper, scale_at(-LANES), 0.0)

    for way in range(2):
        start_if(way, rim_copy(way))
    send_chunk(ORDER[2])
    send_direct()
    for way in range(2):

        @pl.when(sent[way] & jnp.logical_not(passes[way]))
        def _():
            chunk_copy(way, ORDER[3]).start()

    def absorb(chunk, first=False, last_one=False):
        def place(variables):
            for var in variables:
                moved = jnp.concatenate([recv[0, chunk, var], recv[1, chunk, var]], axis=0)
                nodal[var, pl.ds(chunk * LANES, LANES), :] = (rows_at(chunk, var, 0, LANES) + moved).T

        if chunk == ORDER[3]:
            for way in range(2):
                finish(way, piece_copy(way), recv.at[way, chunk, pl.ds(0, PIECE)])
            place(range(PIECE))
            for way in range(2):
                finish(way, chunk_copy(way, chunk), recv.at[way, chunk, pl.ds(PIECE, VARS - PIECE)])
            place(range(PIECE, VARS))
        else:
            for way in range(2):
                finish(way, chunk_copy(way, chunk), recv.at[way, chunk])
            place(range(VARS))
        for part in range(8):
            rows = pl.ds(chunk * LANES + part * 16, 16)
            state = [nodal[var, rows, :] for var in range(VARS)]
            momenta = state[1:4]
            inverse = 1.0 / state[0]
            velocity = [item * inverse for item in momenta]
            product = [[None] * 3 for _ in range(3)]
            for row in range(3):
                for col in range(row, 3):
                    product[row][col] = product[col][row] = momenta[row] * velocity[col]
            kinetic = 0.5 * (product[0][0] + product[1][1] + product[2][2])
            pressure = (GAMMA - 1.0) * (state[4] - kinetic)
            enthalpy = state[4] + pressure
            square = GAMMA * pressure * inverse
            sound = square * lax.rsqrt(square)
            for axis_dir, target in enumerate((flux_x, flux_y, flux_z)):
                target[0, rows, :] = momenta[axis_dir]
                for other in range(3):
                    value = product[axis_dir][other]
                    target[1 + other, rows, :] = value + pressure if other == axis_dir else value
                target[4, rows, :] = enthalpy * velocity[axis_dir]
                if axis_dir < 2:
                    speeds[axis_dir, rows, :] = jnp.abs(velocity[axis_dir]) + sound
        layers = (2 * chunk, 2 * chunk + 1)
        for side in range(2):
            for layer in layers:
                for var in range(VARS):
                    ends_z[side, var, pl.ds(layer * 8, 8), :] = nodal[
                        var, at_rows(trace_rows(4 + side, layer)), :
                    ]
        if not last_one:
            differentiate(chunk, first)

    def differentiate(chunk, first=False, last_one=False):
        layers = (2 * chunk, 2 * chunk + 1)
        for var in range(VARS):
            for layer in layers:
                base = layer * 64
                rows = [pl.ds(base + place, 8, stride=8) for place in range(8)]
                parts = derivative(matrix, [flux_z[var, rows[place], :] for place in range(8)])
                for place in range(8):
                    slope_z[var, rows[place], :] = parts[place]
            along_y = [
                derivative(matrix, [flux_y[var, pl.ds(layer * 64 + 8 * place, 8), :] for place in range(8)])
                for layer in layers
            ]
            for group in range(8):
                values = [flux_x[var, pl.ds(layer * 64 + 8 * group, 8), :] for layer in layers]
                for target in layers if last_one else range(8):
                    rows = pl.ds(target * 64 + 8 * group, 8)
                    terms = [] if first else [total[var, rows, :]]
                    if not last_one:
                        terms += [float(matrix[target, layer]) * value for layer, value in zip(layers, values)]
                    if target in layers:
                        terms += [along_y[target - layers[0]][group], slope_z[var, rows, :]]
                    total[var, rows, :] = functools.reduce(lambda left, right: left + right, terms)

    def across(face_id):
        partner = jnp.broadcast_to(partner_ref[pl.ds(face_id, 1), :], (8, LANES))
        return partner, partner & 127

    def fetch_layers(face_ids, layers):
        for face_id in face_ids:
            partner, local = across(face_id)
            away = (partner >> 7) != me
            for layer in layers:
                for var in range(VARS):
                    if face_id < 4:
                        value = nodal[var, at_rows(trace_rows(face_id ^ 1, layer)), :]
                    else:
                        value = ends_z[5 - face_id, var, pl.ds(layer * 8, 8), :]
                    value = pick(value, local, 1)
                    if face_id >= 4:
                        index = (partner & 7) + var * 8 + (0 if face_id == 4 else 64)
                        other = jnp.where(
                            (partner & 8) == 0,
                            pick(rim_turned[pl.ds(layer * 8, 8), :], index, 1),
                            pick(rim_turned[pl.ds(64 + layer * 8, 8), :], index, 1),
                        )
                        value = jnp.where(away, other, value)
                    fetched[face_id, var, pl.ds(layer * 8, 8), :] = value

    row8 = lax.broadcasted_iota(jnp.int32, (8, LANES), 0)

    def correct(face_id):
        axis_dir, sign_out = face_id // 2, 1.0 if face_id % 2 else -1.0
        partner, _ = across(face_id)
        code = jnp.broadcast_to(orient_ref[pl.ds(face_id, 1), :], (8, LANES))
        turned = code >= 4
        flip_first = (code & 2) != 0
        flip_second = jnp.where((code & 1) != 0, 7 - row8, row8)
        wall = partner < 0
        inner_flux = (flux_x, flux_y, None)[axis_dir]
        for layer in range(4):
            pair = (layer, 7 - layer)
            aligned = [[], []]
            for var in range(VARS):
                near, far = [
                    jnp.where(
                        turned,
                        fetched[face_id, var, pl.ds(place, 8, stride=8), :],
                        fetched[face_id, var, pl.ds(place * 8, 8), :],
                    )
                    for place in pair
                ]
                aligned[0].append(pick(jnp.where(flip_first, far, near), flip_second, 0))
                aligned[1].append(pick(jnp.where(flip_first, near, far), flip_second, 0))
            for which in range(2):
                rows = at_rows(trace_rows(face_id, pair[which]))
                outer = aligned[which]
                if axis_dir == 2:
                    layer_rows = pl.ds(pair[which] * 8, 8)
                    inner = [ends_z[face_id - 4, var, layer_rows, :] for var in range(VARS)]
                    outer = [
                        jnp.where(wall, -inner[var] if var == 1 + axis_dir else inner[var], outer[var])
                        for var in range(VARS)
                    ]
                    flux_in, speed_in = side_terms(inner, axis_dir)
                else:
                    inner = [nodal[var, rows, :] for var in range(VARS)]
                    flux_in = [inner_flux[var, rows, :] for var in range(VARS)]
                    speed_in = speeds[axis_dir, rows, :]
                flux_out, speed_out = side_terms(outer, axis_dir)
                wave = jnp.maximum(speed_in, speed_out)
                for var in range(VARS):
                    jump = flux_out[var] - flux_in[var] if sign_out > 0 else flux_in[var] - flux_out[var]
                    total[var, rows, :] = total[var, rows, :] + (jump - wave * (outer[var] - inner[var]))

    def layers_of(chunks):
        return [layer for chunk in chunks for layer in (2 * chunk, 2 * chunk + 1)]

    absorb(ORDER[0], first=True)
    pass_on()
    absorb(ORDER[1])
    fetch_layers((0, 1), range(8))
    correct(0)
    correct(1)
    fetch_layers((2, 3), layers_of(ORDER[:2]))
    for way in range(2):
        finish(way, rim_copy(way), rim_recv.at[way])
    scale = scale_at(0) + rim_recv[0, last, :] + rim_recv[1, last, :]
    traces = pl.ds(0, VARS * 8)
    blank = jnp.zeros((64 - VARS * 8, LANES), jnp.float32)
    rim_turned[...] = jnp.concatenate(
        [
            rim_own[0] + rim_recv[0, traces, :],
            blank,
            rim_own[1] + rim_recv[1, traces, :],
            blank,
        ],
        axis=0,
    ).T
    fetch_layers((4, 5), layers_of(ORDER[:2]))
    absorb(ORDER[2])
    fetch_layers((2, 3, 4, 5), layers_of(ORDER[2:3]))
    absorb(ORDER[3], last_one=True)
    fetch_layers((4, 5, 2, 3), layers_of(ORDER[3:]))
    for face_id in (4, 5):
        correct(face_id)
    differentiate(ORDER[3], last_one=True)
    for face_id in (2, 3):
        correct(face_id)

    factor = jnp.broadcast_to((-TIME_STEP * lift) * scale[:1, :], (64, LANES))
    late = layers_of(ORDER[3:])
    for var in range(VARS):
        values = [flux_x[var, pl.ds(layer * 64, 64), :] for layer in late]
        for chunk in range(CHUNKS):
            blocks = []
            for target in layers_of((chunk,)):
                rows = pl.ds(target * 64, 64)
                slope = total[var, rows, :]
                for layer, value in zip(late, values):
                    slope = slope + float(matrix[target, layer]) * value
                blocks.append(nodal[var, rows, :] + factor * slope)
            result[var, :, pl.ds(chunk * LANES, LANES)] = jnp.concatenate(blocks, axis=0).T
    for way in range(2):

        @pl.when(sent[way])
        def _():
            for chunk in range(CHUNKS):
                chunk_copy(way, chunk).wait_send()
            piece_copy(way).wait_send()
            rim_copy(way).wait_send()

        @pl.when(passes[way])
        def _():
            passed_copy(way).wait_send()


def body(state_old, metric_old, new_position, partner, orient):
    matrix, weights = node_tables(POINTS)
    nodes = state_old.shape[2]
    rows_dev = partner.shape[1]
    cube = pltpu.VMEM((VARS, nodes, LANES), jnp.float32)
    advanced = pl.pallas_call(
        functools.partial(kernel, matrix * (2.0 * weights[0]), float(0.5 / weights[0])),
        out_shape=jax.ShapeDtypeStruct((VARS, rows_dev, nodes), jnp.float32),
        in_specs=[pl.BlockSpec(memory_space=pltpu.HBM)] * 6,
        out_specs=pl.BlockSpec(memory_space=pltpu.VMEM),
        scratch_shapes=[
            pltpu.SMEM((256,), jnp.int32),
            pltpu.VMEM((2, LANES), jnp.int32),
            pltpu.VMEM((2, LANES), jnp.float32),
            pltpu.VMEM((6, LANES), jnp.int32),
            pltpu.VMEM((6, LANES), jnp.int32),
        ]
        + [pltpu.VMEM((VARS, 2 * PAD, LANES), jnp.float32)] * CHUNKS
        + [
            pltpu.VMEM((2, CHUNKS, VARS, 64, LANES), jnp.float32),
            pltpu.VMEM((2, CHUNKS, VARS, 64, LANES), jnp.float32),
            pltpu.VMEM((2, VARS * 8 + 8, LANES), jnp.float32),
            pltpu.VMEM((2, VARS * 8 + 8, LANES), jnp.float32),
            pltpu.VMEM((2, VARS * 8, LANES), jnp.float32),
            pltpu.VMEM((LANES, LANES), jnp.float32),
        ]
        + [cube] * 6
        + [
            pltpu.VMEM((2, VARS, 64, LANES), jnp.float32),
            pltpu.VMEM((2, nodes, LANES), jnp.float32),
            pltpu.VMEM((6, VARS, 64, LANES), jnp.float32),
            pltpu.SemaphoreType.DMA((CHUNKS,)),
            pltpu.SemaphoreType.DMA((5,)),
            pltpu.SemaphoreType.DMA((2, CHUNKS + 1)),
            pltpu.SemaphoreType.DMA((2, CHUNKS + 1)),
            pltpu.SemaphoreType.DMA((2,)),
            pltpu.SemaphoreType.DMA((2,)),
            pltpu.VMEM((PIECE, 64, LANES), jnp.float32),
            pltpu.SemaphoreType.DMA((2,)),
        ],
        compiler_params=pltpu.CompilerParams(
            collective_id=0, has_side_effects=True, vmem_limit_bytes=VMEM_LIMIT
        ),
    )(
        *[
            pltpu.with_memory_space_constraint(item, pltpu.HBM)
            for item in (
                new_position,
                new_position.reshape(2, LANES),
                metric_old.reshape(2, LANES),
                partner,
                orient,
                state_old.transpose(1, 0, 2),
            )
        ]
    )
    return advanced.transpose(1, 0, 2)


def solution(mesh):
    placed = (
        P(("curve", "sub"), None, None),
        P(("curve", "sub")),
        P(("curve", "sub")),
        P(None, ("curve", "sub")),
        P(None, ("curve", "sub")),
    )
    return jax.shard_map(
        body, mesh=mesh, in_specs=placed, out_specs=P(("curve", "sub"), None, None), check_vma=False
    )
```

```python
import functools

import jax
import jax.numpy as jnp
import numpy as np
from jax import lax
from jax.experimental import pallas as pl
from jax.experimental.pallas import tpu as pltpu
from jax.sharding import PartitionSpec as P

POINTS = 8
RIM = 16
VARS = 5
GAMMA = 1.4
TIME_STEP = 0.002
MESH = pl.DeviceIdType.MESH
CHUNKS = 4
ORDER = (0, 3, 1, 2)
PAD = 320
PIECE = 3
VMEM_LIMIT = 50 * 1024 * 1024
LANES = 128


def legendre_values(points, degree):
    previous = np.ones(points.shape)
    current = points.copy()
    for order_id in range(2, degree + 1):
        following = ((2 * order_id - 1) * points * current - (order_id - 1) * previous) / order_id
        previous = current
        current = following
    return (current, previous)


def lobatto_points(degree):
    points = np.cos(np.pi * np.arange(degree + 1) / degree)
    for sweep_id in range(100):
        current, previous = legendre_values(points, degree)
        points = points - (points * current - previous) / ((degree + 1) * current)
    points = points[::-1].copy()
    points[0] = -1.0
    points[degree] = 1.0
    return points


def node_tables(num_points):
    degree = num_points - 1
    points = lobatto_points(degree)
    values = legendre_values(points, degree)[0]
    weights = 2.0 / (degree * (degree + 1) * values**2)
    matrix = np.zeros((num_points, num_points))
    for row_pos in range(num_points):
        for col_pos in range(num_points):
            if row_pos != col_pos:
                matrix[row_pos, col_pos] = values[row_pos] / (
                    values[col_pos] * (points[row_pos] - points[col_pos])
                )
    matrix[0, 0] = -degree * (degree + 1) / 4.0
    matrix[degree, degree] = degree * (degree + 1) / 4.0
    return (matrix, weights)


def derivative(matrix, values):
    evens = [values[place] + values[7 - place] for place in range(4)]
    odds = [values[place] - values[7 - place] for place in range(4)]
    first, second = [], []
    for row in range(4):
        even, odd = [
            functools.reduce(
                lambda left, right: left + right,
                [
                    float(0.5 * (matrix[row, col] + sign * matrix[row, 7 - col])) * items[col]
                    for col in range(4)
                ],
            )
            for sign, items in ((1.0, evens), (-1.0, odds))
        ]
        first.append(even + odd)
        second.append(odd - even)
    return first + second[::-1]


def pick(values, index, axis):
    other = 1 - axis
    numbers = lax.GatherDimensionNumbers(
        offset_dims=(),
        collapsed_slice_dims=(axis,),
        start_index_map=(axis,),
        operand_batching_dims=(other,),
        start_indices_batching_dims=(other,),
    )
    return lax.gather(
        values, index[..., None], numbers, (1, 1), mode=lax.GatherScatterMode.PROMISE_IN_BOUNDS
    )


def trace_rows(face_id, layer):
    edge = 0 if face_id % 2 == 0 else POINTS - 1
    return ((edge * 64 + layer * 8, 1), (layer * 64 + edge * 8, 1), (layer * 64 + edge, 8))[face_id // 2]


def at_rows(rows):
    first, stride = rows
    return pl.ds(first, 8) if stride == 1 else pl.ds(first, 8, stride=stride)


def side_terms(state, axis_dir):
    inverse = 1.0 / state[0]
    momenta = state[1:4]
    kinetic = 0.5 * inverse * (momenta[0] * momenta[0] + momenta[1] * momenta[1] + momenta[2] * momenta[2])
    pressure = (GAMMA - 1.0) * (state[4] - kinetic)
    normal = momenta[axis_dir] * inverse
    square = GAMMA * pressure * inverse
    speed = jnp.abs(normal) + square * lax.rsqrt(square)
    flux = [momenta[axis_dir]] + [item * normal for item in momenta] + [(state[4] + pressure) * normal]
    flux[1 + axis_dir] = flux[1 + axis_dir] + pressure
    return flux, speed


def kernel(
    matrix,
    lift,
    position_row_hbm,
    position_hbm,
    metric_hbm,
    partner_hbm,
    orient_hbm,
    state_hbm,
    result,
    first_ref,
    position_ref,
    metric_ref,
    partner_ref,
    orient_ref,
    staged_0,
    staged_1,
    staged_2,
    staged_3,
    send,
    recv,
    rim_send,
    rim_recv,
    rim_own,
    rim_turned,
    nodal,
    total,
    flux_x,
    flux_y,
    flux_z,
    slope_z,
    ends_z,
    speeds,
    fetched,
    in_sem,
    table_sem,
    send_sem,
    recv_sem,
    rim_send_sem,
    rim_recv_sem,
    passing,
    pass_sem,
):
    sub_size = lax.axis_size("sub")
    devices = lax.axis_size("curve") * sub_size
    me = lax.axis_index("curve") * sub_size + lax.axis_index("sub")
    has_next, has_prev = me < devices - 1, me > 0
    after, before = jnp.minimum(me + 1, devices - 1), jnp.maximum(me - 1, 0)
    sides = ((after // sub_size, lax.rem(after, sub_size)), (before // sub_size, lax.rem(before, sub_size)))
    sent, arrives = (has_next, has_prev), (has_prev, has_next)

    plane = lax.axis_size("curve") * sub_size // 4
    spot_id, level = lax.rem(me, plane), me // plane
    is_low = (spot_id == plane - 1) & (level < 3)
    is_high = (spot_id == 0) & (level > 0)
    pass_up = (spot_id == sub_size - 1) & (level > 0)
    pass_down = (spot_id == plane - sub_size) & (level < 3)
    detours = (is_low, is_high)
    passes = (pass_up, pass_down)

    def mesh_place(device):
        device = jnp.clip(device, 0, devices - 1)
        return (device // sub_size, lax.rem(device, sub_size))

    passers = (mesh_place(me + sub_size), mesh_place(me - sub_size))
    sources = (mesh_place(me - sub_size), mesh_place(me + sub_size))
    drains = (mesh_place(me - sub_size + 1), mesh_place(me + sub_size - 1))
    fillers = (mesh_place(me + sub_size - 1), mesh_place(me - sub_size + 1))

    barrier = pltpu.get_barrier_semaphore()
    for way in range(2):

        @pl.when(sent[way])
        def _():
            pl.semaphore_signal(barrier, inc=1, device_id=sides[way], device_id_type=MESH)

        @pl.when(passes[way])
        def _():
            pl.semaphore_signal(barrier, inc=1, device_id=sources[way], device_id_type=MESH)

        @pl.when(detours[1 - way])
        def _():
            pl.semaphore_signal(barrier, inc=1, device_id=fillers[way], device_id_type=MESH)

    tables = [
        pltpu.make_async_copy(source, target, table_sem.at[place])
        for place, (source, target) in enumerate(
            (
                (position_row_hbm, first_ref),
                (position_hbm, position_ref),
                (metric_hbm, metric_ref),
                (partner_hbm, partner_ref),
                (orient_hbm, orient_ref),
            )
        )
    ]
    for copy in tables[:2]:
        copy.start()
    staged = (staged_0, staged_1, staged_2, staged_3)
    loads = [
        pltpu.make_async_copy(
            state_hbm.at[:, :, pl.ds(chunk * LANES, LANES)],
            staged[chunk].at[:, pl.ds(PAD, 256), :],
            in_sem.at[chunk],
        )
        for chunk in range(CHUNKS)
    ]
    for chunk in (ORDER[3],) + ORDER[:3]:
        loads[chunk].start()
    for copy in tables[2:]:
        copy.start()
    for copy in tables[:2]:
        copy.wait()

    shift = me * LANES - first_ref[0]
    start = PAD + jnp.clip(shift, -255, 128)
    alive = jnp.where(position_ref[...] >= 0, 1.0, 0.0)
    count = jnp.sum(alive).astype(jnp.int32)
    low, high = -shift, count - shift

    def rows_at(chunk, var, local, size):
        block = staged[chunk][var, pl.ds(start + local, size), :]
        row = local + lax.broadcasted_iota(jnp.int32, (size, LANES), 0)
        return jnp.where((row >= low) & (row < high), block, 0.0)

    def to_side(source, target, send_sems, recv_sems, way):
        return pltpu.make_async_remote_copy(
            src_ref=source,
            dst_ref=target,
            send_sem=send_sems,
            recv_sem=recv_sems,
            device_id=sides[way],
            device_id_type=MESH,
        )

    def start_if(way, copy):
        @pl.when(sent[way])
        def _():
            copy.start()

    def finish(way, copy, target):
        @pl.when(arrives[way])
        def _():
            copy.wait_recv()

        @pl.when(jnp.logical_not(arrives[way]))
        def _():
            target[...] = jnp.zeros(target.shape, jnp.float32)

    def chunk_copy(way, chunk):
        place = (way, chunk, pl.ds(PIECE, VARS - PIECE)) if chunk == ORDER[3] else (way, chunk)
        return to_side(send.at[place], recv.at[place], send_sem.at[way, chunk], recv_sem.at[way, chunk], way)

    def piece_copy(way, target=None, target_sem=None, device=None):
        place = (way, ORDER[3], pl.ds(0, PIECE))
        return pltpu.make_async_remote_copy(
            src_ref=send.at[place],
            dst_ref=recv.at[place] if target is None else target,
            send_sem=send_sem.at[way, CHUNKS],
            recv_sem=recv_sem.at[way, CHUNKS] if target is None else target_sem,
            device_id=sides[way] if target is None else device,
            device_id_type=MESH,
        )

    def send_detours():
        for way in range(2):

            @pl.when(detours[way])
            def _():
                piece_copy(way, passing, pass_sem.at[0], passers[way]).start()

    def send_direct():
        for way in range(2):

            @pl.when(sent[way] & jnp.logical_not(detours[way]))
            def _():
                piece_copy(way).start()

    def passed_copy(way):
        return pltpu.make_async_remote_copy(
            src_ref=passing,
            dst_ref=recv.at[way, ORDER[3], pl.ds(0, PIECE)],
            send_sem=pass_sem.at[1],
            recv_sem=recv_sem.at[way, CHUNKS],
            device_id=drains[way],
            device_id_type=MESH,
        )

    def pass_on():
        for way in range(2):

            @pl.when(passes[way])
            def _():
                piece_copy(way, passing, pass_sem.at[0], sides[way]).wait_recv()
                passed_copy(way).start()
                chunk_copy(way, ORDER[3]).start()

    def rim_copy(way):
        return to_side(rim_send.at[way], rim_recv.at[way], rim_send_sem.at[way], rim_recv_sem.at[way], way)

    def send_chunk(chunk):
        for way in range(2):
            start_if(way, chunk_copy(way, chunk))

    def build(chunk):
        loads[chunk].wait()
        for way, local in ((0, LANES), (1, -64)):
            for var in range(VARS):
                send[way, chunk, var] = rows_at(chunk, var, local, 64)

    build(ORDER[3])
    build(ORDER[0])
    peers = [has_next, has_prev, is_low, is_high, pass_up, pass_down]
    pl.semaphore_wait(barrier, sum([peer.astype(jnp.int32) for peer in peers], jnp.int32(0)))
    send_detours()
    send_chunk(ORDER[0])
    build(ORDER[1])
    send_chunk(ORDER[1])
    build(ORDER[2])
    for copy in tables[2:]:
        copy.wait()

    lane8 = lax.broadcasted_iota(jnp.int32, (8, LANES), 1)
    upper = lane8 >= 64
    piece = lax.rem(lane8, 64) // 16
    bottom = lax.rem(lane8, 16) * 8
    top = bottom + POINTS - 1
    for target, local, spot in (
        (rim_send.at[0], LANES - RIM, top),
        (rim_send.at[1], 0, bottom),
        (rim_own.at[0], -RIM, top),
        (rim_own.at[1], LANES, bottom),
    ):
        for var in range(VARS):
            value = None
            for chunk in range(CHUNKS):
                rows = rows_at(chunk, var, local, RIM)
                part = jnp.where(upper, pick(rows[8:], spot, 1), pick(rows[:8], spot, 1))
                value = part if value is None else jnp.where(piece == chunk, part, value)
            target[pl.ds(var * 8, 8), :] = value

    halves = [jnp.broadcast_to(metric_ref[pl.ds(half, 1), :], (8, LANES)) for half in range(2)]

    def scale_at(local):
        row = local + lane8
        index = row + shift
        value = jnp.where(index < LANES, pick(halves[0], index & 127, 1), pick(halves[1], index & 127, 1))
        return jnp.where((row >= low) & (row < high), value, 0.0)

    last = pl.ds(VARS * 8, 8)
    rim_send[0, last, :] = jnp.where(upper, 0.0, scale_at(LANES))
    rim_send[1, last, :] = jnp.where(upper, scale_at(-LANES), 0.0)

    for way in range(2):
        start_if(way, rim_copy(way))
    send_chunk(ORDER[2])
    send_direct()
    for way in range(2):

        @pl.when(sent[way] & jnp.logical_not(passes[way]))
        def _():
            chunk_copy(way, ORDER[3]).start()

    def absorb(chunk, first=False, last_one=False):
        def place(variables):
            for var in variables:
                moved = jnp.concatenate([recv[0, chunk, var], recv[1, chunk, var]], axis=0)
                nodal[var, pl.ds(chunk * LANES, LANES), :] = (rows_at(chunk, var, 0, LANES) + moved).T

        if chunk == ORDER[3]:
            for way in range(2):
                finish(way, piece_copy(way), recv.at[way, chunk, pl.ds(0, PIECE)])
            place(range(PIECE))
            for way in range(2):
                finish(way, chunk_copy(way, chunk), recv.at[way, chunk, pl.ds(PIECE, VARS - PIECE)])
            place(range(PIECE, VARS))
        else:
            for way in range(2):
                finish(way, chunk_copy(way, chunk), recv.at[way, chunk])
            place(range(VARS))
        for part in range(8):
            rows = pl.ds(chunk * LANES + part * 16, 16)
            state = [nodal[var, rows, :] for var in range(VARS)]
            momenta = state[1:4]
            inverse = 1.0 / state[0]
            velocity = [item * inverse for item in momenta]
            product = [[None] * 3 for _ in range(3)]
            for row in range(3):
                for col in range(row, 3):
                    product[row][col] = product[col][row] = momenta[row] * velocity[col]
            kinetic = 0.5 * (product[0][0] + product[1][1] + product[2][2])
            pressure = (GAMMA - 1.0) * (state[4] - kinetic)
            enthalpy = state[4] + pressure
            square = GAMMA * pressure * inverse
            sound = square * lax.rsqrt(square)
            for axis_dir, target in enumerate((flux_x, flux_y, flux_z)):
                target[0, rows, :] = momenta[axis_dir]
                for other in range(3):
                    value = product[axis_dir][other]
                    target[1 + other, rows, :] = value + pressure if other == axis_dir else value
                target[4, rows, :] = enthalpy * velocity[axis_dir]
                if axis_dir < 2:
                    speeds[axis_dir, rows, :] = jnp.abs(velocity[axis_dir]) + sound
        layers = (2 * chunk, 2 * chunk + 1)
        for side in range(2):
            for layer in layers:
                for var in range(VARS):
                    ends_z[side, var, pl.ds(layer * 8, 8), :] = nodal[
                        var, at_rows(trace_rows(4 + side, layer)), :
                    ]
        if not last_one:
            differentiate(chunk, first)

    def differentiate(chunk, first=False, last_one=False):
        layers = (2 * chunk, 2 * chunk + 1)
        for var in range(VARS):
            for layer in layers:
                base = layer * 64
                rows = [pl.ds(base + place, 8, stride=8) for place in range(8)]
                parts = derivative(matrix, [flux_z[var, rows[place], :] for place in range(8)])
                for place in range(8):
                    slope_z[var, rows[place], :] = parts[place]
            along_y = [
                derivative(matrix, [flux_y[var, pl.ds(layer * 64 + 8 * place, 8), :] for place in range(8)])
                for layer in layers
            ]
            for group in range(8):
                values = [flux_x[var, pl.ds(layer * 64 + 8 * group, 8), :] for layer in layers]
                for target in layers if last_one else range(8):
                    rows = pl.ds(target * 64 + 8 * group, 8)
                    terms = [] if first else [total[var, rows, :]]
                    if not last_one:
                        terms += [float(matrix[target, layer]) * value for layer, value in zip(layers, values)]
                    if target in layers:
                        terms += [along_y[target - layers[0]][group], slope_z[var, rows, :]]
                    total[var, rows, :] = functools.reduce(lambda left, right: left + right, terms)

    def across(face_id):
        partner = jnp.broadcast_to(partner_ref[pl.ds(face_id, 1), :], (8, LANES))
        return partner, partner & 127

    def fetch_layers(face_ids, layers):
        for face_id in face_ids:
            partner, local = across(face_id)
            away = (partner >> 7) != me
            for layer in layers:
                for var in range(VARS):
                    if face_id < 4:
                        value = nodal[var, at_rows(trace_rows(face_id ^ 1, layer)), :]
                    else:
                        value = ends_z[5 - face_id, var, pl.ds(layer * 8, 8), :]
                    value = pick(value, local, 1)
                    if face_id >= 4:
                        index = (partner & 7) + var * 8 + (0 if face_id == 4 else 64)
                        other = jnp.where(
                            (partner & 8) == 0,
                            pick(rim_turned[pl.ds(layer * 8, 8), :], index, 1),
                            pick(rim_turned[pl.ds(64 + layer * 8, 8), :], index, 1),
                        )
                        value = jnp.where(away, other, value)
                    fetched[face_id, var, pl.ds(layer * 8, 8), :] = value

    row8 = lax.broadcasted_iota(jnp.int32, (8, LANES), 0)

    def correct(face_id):
        axis_dir, sign_out = face_id // 2, 1.0 if face_id % 2 else -1.0
        partner, _ = across(face_id)
        code = jnp.broadcast_to(orient_ref[pl.ds(face_id, 1), :], (8, LANES))
        turned = code >= 4
        flip_first = (code & 2) != 0
        flip_second = jnp.where((code & 1) != 0, 7 - row8, row8)
        wall = partner < 0
        inner_flux = (flux_x, flux_y, None)[axis_dir]
        for layer in range(4):
            pair = (layer, 7 - layer)
            aligned = [[], []]
            for var in range(VARS):
                near, far = [
                    jnp.where(
                        turned,
                        fetched[face_id, var, pl.ds(place, 8, stride=8), :],
                        fetched[face_id, var, pl.ds(place * 8, 8), :],
                    )
                    for place in pair
                ]
                aligned[0].append(pick(jnp.where(flip_first, far, near), flip_second, 0))
                aligned[1].append(pick(jnp.where(flip_first, near, far), flip_second, 0))
            for which in range(2):
                rows = at_rows(trace_rows(face_id, pair[which]))
                outer = aligned[which]
                if axis_dir == 2:
                    layer_rows = pl.ds(pair[which] * 8, 8)
                    inner = [ends_z[face_id - 4, var, layer_rows, :] for var in range(VARS)]
                    outer = [
                        jnp.where(wall, -inner[var] if var == 1 + axis_dir else inner[var], outer[var])
                        for var in range(VARS)
                    ]
                    flux_in, speed_in = side_terms(inner, axis_dir)
                else:
                    inner = [nodal[var, rows, :] for var in range(VARS)]
                    flux_in = [inner_flux[var, rows, :] for var in range(VARS)]
                    speed_in = speeds[axis_dir, rows, :]
                flux_out, speed_out = side_terms(outer, axis_dir)
                wave = jnp.maximum(speed_in, speed_out)
                for var in range(VARS):
                    jump = flux_out[var] - flux_in[var] if sign_out > 0 else flux_in[var] - flux_out[var]
                    total[var, rows, :] = total[var, rows, :] + (jump - wave * (outer[var] - inner[var]))

    def layers_of(chunks):
        return [layer for chunk in chunks for layer in (2 * chunk, 2 * chunk + 1)]

    absorb(ORDER[0], first=True)
    pass_on()
    absorb(ORDER[1])
    fetch_layers((0, 1), range(8))
    correct(0)
    correct(1)
    fetch_layers((2, 3), layers_of(ORDER[:2]))
    for way in range(2):
        finish(way, rim_copy(way), rim_recv.at[way])
    scale = scale_at(0) + rim_recv[0, last, :] + rim_recv[1, last, :]
    traces = pl.ds(0, VARS * 8)
    blank = jnp.zeros((64 - VARS * 8, LANES), jnp.float32)
    rim_turned[...] = jnp.concatenate(
        [
            rim_own[0] + rim_recv[0, traces, :],
            blank,
            rim_own[1] + rim_recv[1, traces, :],
            blank,
        ],
        axis=0,
    ).T
    fetch_layers((4, 5), layers_of(ORDER[:2]))
    absorb(ORDER[2])
    fetch_layers((2, 3, 4, 5), layers_of(ORDER[2:3]))
    absorb(ORDER[3], last_one=True)
    fetch_layers((4, 5), layers_of(ORDER[3:]))
    for face_id in (4, 5):
        correct(face_id)
    fetch_layers((2, 3), layers_of(ORDER[3:]))
    differentiate(ORDER[3], last_one=True)
    for face_id in (2, 3):
        correct(face_id)

    factor = jnp.broadcast_to((-TIME_STEP * lift) * scale[:1, :], (64, LANES))
    late = layers_of(ORDER[3:])
    for var in range(VARS):
        values = [flux_x[var, pl.ds(layer * 64, 64), :] for layer in late]
        for chunk in range(CHUNKS):
            blocks = []
            for target in layers_of((chunk,)):
                rows = pl.ds(target * 64, 64)
                slope = total[var, rows, :]
                for layer, value in zip(late, values):
                    slope = slope + float(matrix[target, layer]) * value
                blocks.append(nodal[var, rows, :] + factor * slope)
            result[var, :, pl.ds(chunk * LANES, LANES)] = jnp.concatenate(blocks, axis=0).T
    for way in range(2):

        @pl.when(sent[way])
        def _():
            for chunk in range(CHUNKS):
                chunk_copy(way, chunk).wait_send()
            piece_copy(way).wait_send()
            rim_copy(way).wait_send()

        @pl.when(passes[way])
        def _():
            passed_copy(way).wait_send()


def body(state_old, metric_old, new_position, partner, orient):
    matrix, weights = node_tables(POINTS)
    nodes = state_old.shape[2]
    rows_dev = partner.shape[1]
    cube = pltpu.VMEM((VARS, nodes, LANES), jnp.float32)
    advanced = pl.pallas_call(
        functools.partial(kernel, matrix * (2.0 * weights[0]), float(0.5 / weights[0])),
        out_shape=jax.ShapeDtypeStruct((VARS, rows_dev, nodes), jnp.float32),
        in_specs=[pl.BlockSpec(memory_space=pltpu.HBM)] * 6,
        out_specs=pl.BlockSpec(memory_space=pltpu.VMEM),
        scratch_shapes=[
            pltpu.SMEM((256,), jnp.int32),
            pltpu.VMEM((2, LANES), jnp.int32),
            pltpu.VMEM((2, LANES), jnp.float32),
            pltpu.VMEM((6, LANES), jnp.int32),
            pltpu.VMEM((6, LANES), jnp.int32),
        ]
        + [pltpu.VMEM((VARS, 2 * PAD, LANES), jnp.float32)] * CHUNKS
        + [
            pltpu.VMEM((2, CHUNKS, VARS, 64, LANES), jnp.float32),
            pltpu.VMEM((2, CHUNKS, VARS, 64, LANES), jnp.float32),
            pltpu.VMEM((2, VARS * 8 + 8, LANES), jnp.float32),
            pltpu.VMEM((2, VARS * 8 + 8, LANES), jnp.float32),
            pltpu.VMEM((2, VARS * 8, LANES), jnp.float32),
            pltpu.VMEM((LANES, LANES), jnp.float32),
        ]
        + [cube] * 6
        + [
            pltpu.VMEM((2, VARS, 64, LANES), jnp.float32),
            pltpu.VMEM((2, nodes, LANES), jnp.float32),
            pltpu.VMEM((6, VARS, 64, LANES), jnp.float32),
            pltpu.SemaphoreType.DMA((CHUNKS,)),
            pltpu.SemaphoreType.DMA((5,)),
            pltpu.SemaphoreType.DMA((2, CHUNKS + 1)),
            pltpu.SemaphoreType.DMA((2, CHUNKS + 1)),
            pltpu.SemaphoreType.DMA((2,)),
            pltpu.SemaphoreType.DMA((2,)),
            pltpu.VMEM((PIECE, 64, LANES), jnp.float32),
            pltpu.SemaphoreType.DMA((2,)),
        ],
        compiler_params=pltpu.CompilerParams(
            collective_id=0, has_side_effects=True, vmem_limit_bytes=VMEM_LIMIT
        ),
    )(
        *[
            pltpu.with_memory_space_constraint(item, pltpu.HBM)
            for item in (
                new_position,
                new_position.reshape(2, LANES),
                metric_old.reshape(2, LANES),
                partner,
                orient,
                state_old.transpose(1, 0, 2),
            )
        ]
    )
    return advanced.transpose(1, 0, 2)


def solution(mesh):
    placed = (
        P(("curve", "sub"), None, None),
        P(("curve", "sub")),
        P(("curve", "sub")),
        P(None, ("curve", "sub")),
        P(None, ("curve", "sub")),
    )
    return jax.shard_map(
        body, mesh=mesh, in_specs=placed, out_specs=P(("curve", "sub"), None, None), check_vma=False
    )
```
